128 devices in a mesh: ty: 8 (over x, core), tx: 16 (over y, z).
Axes of the slice: x: 4, y: 4, z: 4, core: 2. Of those that a mesh axis runs over, the one named last changes fastest.
Arguments:
- roi_feat: bfloat16 [1536, 14, 14, 256], P(('ty', 'tx')), may hold values from -6 to 6
- pre_one: bfloat16 [1536, 14, 14, 256], P(('ty', 'tx')), may hold values from -6 to 6
- grad_two: bfloat16 [1536, 14, 14, 256], P(('ty', 'tx')), may hold values from -24 to 24
- w_one: bfloat16 [3, 3, 256, 256], replicated, may hold values from -0.125 to 0.125
- w_two: bfloat16 [3, 3, 256, 256], replicated, may hold values from -0.125 to 0.125
- roi_rows: bfloat16 [1536, 16, 14], P(('ty', 'tx')), may hold values from -1.5 to 1.5
- roi_cols: bfloat16 [1536, 16, 14], P(('ty', 'tx')), may hold values from -1.5 to 1.5
- target_col: int32 [1536, 1], P(('ty', 'tx')), may hold values from 0 to 15; in each aligned block of 12 rows (0 to 11, 12 to 23, ...) at most 2 rows name the same one
- off_row: int32 [1536], P(('ty', 'tx')), may hold values from 0 to 15
- off_col: int32 [1536], P(('ty', 'tx')), may hold values from 0 to 63
- fpn_input: bfloat16 [128, 1024, 256], P('ty', 'tx'), may hold values from -6 to 6
- fpn_grad: bfloat16 [128, 1024, 256], P('ty', 'tx'), may hold values from -6 to 6
- w_fpn: bfloat16 [3, 3, 256, 256], replicated, may hold values from -0.125 to 0.125
Outputs:
- grad_fpn_input: bfloat16 [128, 1024, 256], P('ty', 'tx')
- grad_w_one: float32 [589824], P(('ty', 'tx'))
- grad_w_two: float32 [589824], P(('ty', 'tx'))
- grad_w_fpn: float32 [589824], P(('ty', 'tx'))
The draws below stay inside these ranges and needn't reach their ends.
Inputs may be any that keep to these rules, and one draw needn't show every extreme that they name: `target_col`: at most 2 regions of one device name the same column, and in every draw some device names some column exactly 2 times.
All inputs are finite; a program needn't handle non-finite values.
Results may differ from the reference program's by a relative error of at most 0.0075.
Values may be sent and summed in bfloat16 or wider, within the bound.
A program may use at most 128 MiB of HBM per device.

```python
import math
import jax
import jax.numpy as jnp
import numpy as np
from jax import lax

C = 256
POOL = 14
BOX = 16
R_DEV = 12
TH = 16
TW = 64
CAP = 2
REGIONS = 1536
H = 128
W = 1024
N_TY = 8
N_TX = 16


def set_ends(entries, key, least, high):
    longest = entries.shape.index(max(entries.shape))
    spots = []
    for shift in (0, 1):
        where = [jax.random.randint(jax.random.fold_in(key, axis), (), 0, length) for axis, length in enumerate(entries.shape)]
        where[longest] = (where[longest] + shift) % entries.shape[longest]
        spots.append(tuple(where))
    return entries.at[spots[0]].set(least).at[spots[1]].set(high)


def spiked(drawn, rng, source, target, parts, factor):
    owner, partner = [(jnp.arange(drawn.shape[dim]) // (drawn.shape[dim] // parts)).reshape([-1 if axis == dim else 1 for axis in range(drawn.ndim)]) for dim in (source, target)]
    chosen = jax.random.permutation(rng, parts)[partner]
    strong = (owner == chosen) | (owner == (partner + parts // 2) % parts)
    return jnp.where(strong, factor * drawn, drawn)


def steps_of(stream_key, shape, shards, least, largest):
    loudness, own = 1.0, jax.random.fold_in(stream_key, 6)
    for dim, blocks in shards:
        heights = jnp.exp(jax.random.uniform(jax.random.fold_in(own, dim), (blocks,), jnp.float32, least / len(shards), largest / len(shards)))
        loudness = loudness * jnp.repeat(heights, shape[dim] // blocks).reshape([-1 if axis == dim else 1 for axis in range(len(shape))])
    return loudness


def deal_out(own_key, own, number, rows, number_of, top, reach, lean):
    order = jax.random.permutation(own_key, number_of)
    heavy_load, ordinary = portions_of(number_of, rows * top, reach, lean, True), portions_of(number_of, rows * top, reach, lean, False)
    places = jnp.arange(number_of)

    def named(tallies, offset_by):
        used = int((tallies > 0).sum())
        fixed = max(1, used // 4)
        shifted = fixed + (places - fixed + offset_by * (used - fixed)) % max(1, number_of - fixed)
        return jnp.zeros((number_of,), jnp.int32).at[order[jnp.where(places < fixed, places, shifted)]].set(jnp.asarray(tallies, jnp.int32))

    tallies = jnp.where(number % 4 == 0, named(heavy_load, number // 4), named(ordinary, number - number // 4 - 1))
    mixed = jax.random.permutation(jax.random.fold_in(own, 3), number_of)
    giver, receiver = mixed[0:number_of // 2 * 2:2], mixed[1:number_of // 2 * 2:2]
    room = jnp.minimum(tallies[giver] - 1, reach - tallies[receiver]) // 2
    room = jnp.where((giver == order[0]) | (receiver == order[0]) | (tallies[receiver] == 0), 0, jnp.maximum(room, 0))
    shifted = jax.random.randint(jax.random.fold_in(own, 4), (number_of // 2,), 0, 1 << 20) % (room + 1)
    tallies = tallies.at[giver].add(-shifted).at[receiver].add(shifted)
    labels = jnp.searchsorted(jnp.cumsum(tallies), jnp.arange(rows * top), side="right").astype(jnp.int32)
    table = labels.reshape(top, rows).T
    table = table[jax.random.permutation(jax.random.fold_in(own, 1), rows)]
    offset_by = jax.random.randint(jax.random.fold_in(own, 2), (rows, 1), 0, top)
    return jnp.take_along_axis(table, (jnp.arange(top)[None, :] + offset_by) % top, axis=1)


def portions_of(amount, total, bound, slope, full):
    loads = [(1 << 20) // math.isqrt(standing ** slope) + 1 for standing in range(1, amount + 1)]
    largest = bound if full else min(bound, max(-(-total // amount), total * loads[0] // sum(loads)))
    least = 1 if total - largest >= amount - 1 else 0
    holding, spare = [largest] + [least] * (amount - 1), total - largest - least * (amount - 1)
    while spare > 0:
        candidates = [i for i in range(1, amount) if holding[i] < largest] or [i for i in range(1, amount) if holding[i] < bound]
        whole, budget = sum([loads[i] for i in candidates]), spare
        for i in candidates:
            addition = min(bound - holding[i], max(1, budget * loads[i] // whole), spare)
            holding[i] = holding[i] + addition
            spare = spare - addition
    return np.array(holding)


def scatter_about(own_key, dims, spread, most, shards=(), kind=jnp.bfloat16):
    loudness = steps_of(own_key, dims, shards, -0.22, 0.18) if shards else 1.0
    entries = jax.random.normal(own_key, dims, jnp.float32) * spread * loudness
    return jnp.minimum(jnp.maximum(entries, -most), most).astype(kind)


def bell_draw_with(rng, dims, width, most, split, heavy, kind=jnp.bfloat16):
    drawn = width * jax.random.normal(rng, dims, jnp.float32)
    if split:
        drawn = drawn * steps_of(rng, dims, split, -0.22, 0.18)
    return jnp.clip(spiked(drawn, jax.random.fold_in(rng, 3), *heavy), -most, most).astype(kind)


def setup_inputs(seed: int = 0) -> dict:
    splits = jax.random.split(jax.random.key(seed), 14)
    roi_feat = scatter_about(splits[0], (REGIONS, POOL, POOL, C), 1.0, 6.0, ((0, 128),))
    pre_one = scatter_about(splits[1], (REGIONS, POOL, POOL, C), 1.0, 6.0, ((0, 128),))
    grad_two = bell_draw_with(splits[2], (REGIONS, POOL, POOL, C), 1.0, 24.0, ((0, 128),), (0, 3, 128, 5.5))
    w_one = scatter_about(splits[3], (3, 3, C, C), (9 * C) ** -0.5, 0.125)
    w_two = scatter_about(splits[4], (3, 3, C, C), (9 * C) ** -0.5, 0.125)
    roi_rows = scatter_about(splits[5], (REGIONS, BOX, POOL), POOL ** -0.5, 1.5, ((0, 128),))
    roi_cols = scatter_about(splits[6], (REGIONS, BOX, POOL), POOL ** -0.5, 1.5, ((0, 128),))
    target_col_keys = jax.random.split(jax.random.fold_in(splits[7], 1), REGIONS // R_DEV)
    target_col_turns = jax.random.permutation(jax.random.fold_in(splits[7], 3), REGIONS // R_DEV)
    target_col = jax.vmap(lambda own, number: deal_out(jax.random.fold_in(splits[7], 2), own, number, R_DEV, N_TX, 1, CAP, 2))(target_col_keys, target_col_turns).reshape((REGIONS, 1))
    off_row = set_ends(jax.random.randint(splits[8], (REGIONS,), 0, TH), jax.random.fold_in(splits[8], 1), 0, TH - 1).astype(jnp.int32)
    off_col = set_ends(jax.random.randint(splits[9], (REGIONS,), 0, TW), jax.random.fold_in(splits[9], 1), 0, TW - 1).astype(jnp.int32)
    fpn_input = scatter_about(splits[10], (H, W, C), 1.0, 6.0, ((0, 8), (1, 16)))
    fpn_grad = bell_draw_with(splits[11], (H, W, C), 1.0, 6.0, ((0, 8), (1, 16)), (0, 2, 8, 2.0))
    w_fpn = scatter_about(splits[12], (3, 3, C, C), (9 * C) ** -0.5, 0.125)
    return dict(roi_feat=roi_feat, pre_one=pre_one, grad_two=grad_two, w_one=w_one, w_two=w_two, roi_rows=roi_rows, roi_cols=roi_cols, target_col=target_col, off_row=off_row, off_col=off_col, fpn_input=fpn_input, fpn_grad=fpn_grad, w_fpn=w_fpn)


def window_patches(padded, row_count, col_count, flipped):
    pieces = []
    for row_step in range(3):
        for col_step in range(3):
            row_start = 2 - row_step if flipped else row_step
            col_start = 2 - col_step if flipped else col_step
            pieces.append(padded[..., row_start:row_start + row_count, col_start:col_start + col_count, :])
    return jnp.concatenate(pieces, axis=-1)


def flipped_weight(weight):
    channels = weight.shape[2]
    return jnp.transpose(weight, (0, 1, 3, 2)).reshape(9 * channels, channels)


def weight_term(gradient, inputs_patch):
    return lax.dot_general(gradient, inputs_patch, (((0,), (0,)), ((), ())), preferred_element_type=jnp.float32)


def region_windows(region_grad, row_weights, col_weights):
    highest = lax.Precision.HIGHEST
    partial_sum = jnp.einsum("nxj,nijc->nixc", col_weights.astype(jnp.float32), region_grad.astype(jnp.float32), precision=highest)
    return jnp.einsum("nyi,nixc->nyxc", row_weights.astype(jnp.float32), partial_sum, precision=highest).astype(jnp.bfloat16)


def reference(roi_feat, pre_one, grad_two, w_one, w_two, roi_rows, roi_cols, target_col, off_row, off_col, fpn_input, fpn_grad, w_fpn):
    region_pad = ((0, 0), (1, 1), (1, 1), (0, 0))
    block_count = REGIONS // R_DEV

    def head_block(totals, block):
        features_in, pre_act, upstream, row_weights, col_weights = block
        positions = R_DEV * POOL * POOL
        active = jnp.maximum(pre_act, 0).astype(jnp.bfloat16)
        back_two = jnp.dot(window_patches(jnp.pad(upstream, region_pad), POOL, POOL, True).reshape(positions, 9 * C), flipped_weight(w_two), preferred_element_type=jnp.float32)
        grad_one = jnp.where(pre_act.reshape(positions, C) > 0, back_two, 0.0).astype(jnp.bfloat16)
        term_two = weight_term(upstream.reshape(positions, C), window_patches(jnp.pad(active, region_pad), POOL, POOL, False).reshape(positions, 9 * C))
        term_one = weight_term(grad_one, window_patches(jnp.pad(features_in, region_pad), POOL, POOL, False).reshape(positions, 9 * C))
        region_grad = jnp.dot(window_patches(jnp.pad(grad_one.reshape(R_DEV, POOL, POOL, C), region_pad), POOL, POOL, True).reshape(positions, 9 * C), flipped_weight(w_one), preferred_element_type=jnp.float32).astype(jnp.bfloat16)
        windows = region_windows(region_grad.reshape(R_DEV, POOL, POOL, C), row_weights, col_weights)
        return (totals[0] + term_one, totals[1] + term_two), windows

    stacked = (roi_feat.reshape(block_count, R_DEV, POOL, POOL, C), pre_one.reshape(block_count, R_DEV, POOL, POOL, C), grad_two.reshape(block_count, R_DEV, POOL, POOL, C), roi_rows.reshape(block_count, R_DEV, BOX, POOL), roi_cols.reshape(block_count, R_DEV, BOX, POOL))
    zero_terms = (jnp.zeros((C, 9 * C), jnp.float32), jnp.zeros((C, 9 * C), jnp.float32))
    (term_one, term_two), windows = lax.scan(head_block, zero_terms, stacked)
    windows = windows.reshape(REGIONS, BOX, BOX, C)

    def add_window(region_at, canvas):
        device = region_at // R_DEV
        row_at = (device // N_TX) * TH + off_row[region_at]
        col_at = target_col[region_at, 0] * TW + off_col[region_at]
        corner_at = (row_at.astype(jnp.int32), col_at.astype(jnp.int32), jnp.int32(0))
        current = lax.dynamic_slice(canvas, corner_at, (BOX, BOX, C))
        return lax.dynamic_update_slice(canvas, current + windows[region_at].astype(canvas.dtype), corner_at)

    canvas = lax.fori_loop(0, REGIONS, add_window, jnp.zeros((H + BOX, W + BOX, C), jnp.float32))
    feature_grad = (fpn_grad.astype(jnp.float32) + canvas[:H, :W]).astype(jnp.bfloat16)
    tile_pad = ((1, 1), (1, 1), (0, 0))
    grad_padded = jnp.pad(feature_grad, tile_pad)
    input_padded = jnp.pad(fpn_input, tile_pad)

    def fpn_block(total, block_at):
        row_at = (block_at * TH).astype(jnp.int32)
        grad_rows = lax.dynamic_slice_in_dim(grad_padded, row_at, TH + 2, 0)
        input_rows = lax.dynamic_slice_in_dim(input_padded, row_at, TH + 2, 0)
        back_rows = jnp.dot(window_patches(grad_rows, TH, W, True).reshape(TH * W, 9 * C), flipped_weight(w_fpn), preferred_element_type=jnp.float32).astype(jnp.bfloat16)
        own_grad = lax.dynamic_slice_in_dim(feature_grad, row_at, TH, 0).reshape(TH * W, C)
        total = total + weight_term(own_grad, window_patches(input_rows, TH, W, False).reshape(TH * W, 9 * C))
        return total, back_rows.reshape(TH, W, C)

    term_fpn, blocks_out = lax.scan(fpn_block, jnp.zeros((C, 9 * C), jnp.float32), jnp.arange(N_TY, dtype=jnp.int32))
    grad_fpn_input = blocks_out.reshape(H, W, C)
    return (grad_fpn_input, term_one.reshape(-1), term_two.reshape(-1), term_fpn.reshape(-1))
```

```python
import functools

import jax
import jax.numpy as jnp
from jax import lax
from jax.experimental import pallas as pl
from jax.experimental.pallas import tpu as pltpu
from jax.sharding import PartitionSpec as P

F32, BF = jnp.float32, jnp.bfloat16
MESH = pl.DeviceIdType.MESH
C = 256
NB, RB = 4, 256
M = NB * RB
TH, TW, PW = 16, 64, 80
FM = TH * PW
FROWS = 16 + 18 * PW + 16
GRP, GR = 32, 144
TN = (((0,), (0,)), ((), ()))
VM = pltpu.CompilerParams(vmem_limit_bytes=60 << 20)


def whole(shape, space=pltpu.VMEM):
    return pl.BlockSpec(memory_space=space)


def fixed(shape):
    zeros = (0,) * len(shape)
    return pl.BlockSpec(shape, lambda *_: zeros, pipeline_mode=pl.Buffered(1))


def load_padded(dst, src, fn=None):
    for r in range(NB):
        for y in range(14):
            v = src[r, y]
            dst[pl.ds(16 + r * RB + y * 16, 14), :] = v if fn is None else fn(v)


def spread(x3, v):
    n = v.shape[0]
    x3[:, 256:512] = v[...]
    x3[pl.ds(1, n - 1), 0:256] = v[pl.ds(0, n - 1), :]
    x3[pl.ds(0, n - 1), 512:768] = v[pl.ds(1, n - 1), :]


def flip_weights(wt, w):
    for dy in range(3):
        for kk in range(3):
            wt[dy, kk * C : (kk + 1) * C, :] = w[dy, 2 - kk].T


def conv_flipped(x3, wt, base, rows, pitch):
    acc = None
    for dy in range(3):
        t = jnp.dot(x3[pl.ds(base + (1 - dy) * pitch, rows), :], wt[dy], preferred_element_type=F32)
        acc = t if acc is None else acc + t
    return acc


def front_kernel(tgt, orow, ocol, pre_ref, g2_ref, w2_ref, w1_ref, rows_ref, cols_ref, win_ref, g1_ref, meta_ref, vb, x3, vp, wt2, wt1):
    step = pl.program_id(0)

    @pl.when(step == 0)
    def _():
        vb[...] = jnp.zeros_like(vb)
        vp[...] = jnp.zeros_like(vp)
        x3[...] = jnp.zeros_like(x3)
        meta_ref[...] = jnp.zeros_like(meta_ref)
        flip_weights(wt2, w2_ref)
        flip_weights(wt1, w1_ref)

    load_padded(vb, g2_ref)
    load_padded(vp, pre_ref)
    spread(x3, vb)
    b2 = conv_flipped(x3, wt2, 16, M, 16)
    g1 = jnp.where(vp[pl.ds(16, M), :] > 0, b2, 0.0).astype(BF)
    g1_ref[...] = g1.reshape(NB, RB, C)
    vb[pl.ds(16, M), :] = g1
    spread(x3, vb)
    rg = conv_flipped(x3, wt1, 16, M, 16).astype(BF)
    lane = lax.broadcasted_iota(jnp.int32, (14, 256), 1)
    bin_ = lax.broadcasted_iota(jnp.int32, (14, 256), 0)
    pick_row = (lax.shift_right_logical(lane, 4) == bin_).astype(BF)
    pick_col = ((lane & 15) == bin_).astype(BF)
    lanes = lax.broadcasted_iota(jnp.int32, (8, 128), 1)
    for r in range(NB):
        rl = jnp.dot(rows_ref[r], pick_row, preferred_element_type=F32)
        cl = jnp.dot(cols_ref[r], pick_col, preferred_element_type=F32)
        both = (rl[:, None, :] * cl[None, :, :]).reshape(256, 256).astype(BF)
        win = jnp.dot(both, rg[r * RB : (r + 1) * RB], preferred_element_type=F32)
        at = step * NB + r
        t = tgt[at]
        k = lax.fori_loop(0, at, lambda q, s: s + jnp.where(tgt[q] == t, 1, 0), 0)
        win_ref[t * 2 + k] = win.astype(BF)
        old = meta_ref[t]
        new = jnp.where(lanes == 4 * k, 1, old)
        new = jnp.where(lanes == 4 * k + 1, orow[at], new)
        meta_ref[t] = jnp.where(lanes == 4 * k + 2, ocol[at], new)


def front(tgt, orow, ocol, pre, g2, w2, w1, rows, cols):
    blk = pl.BlockSpec((NB, 14, 14, C), lambda i, *_: (i, 0, 0, 0))
    rspec = pl.BlockSpec((NB, 16, 14), lambda i, *_: (i, 0, 0))
    return pl.pallas_call(
        front_kernel,
        grid_spec=pltpu.PrefetchScalarGridSpec(
            num_scalar_prefetch=3,
            grid=(3,),
            in_specs=[blk, blk, fixed((3, 3, C, C)), fixed((3, 3, C, C)), rspec, rspec],
            out_specs=[fixed((32, 256, C)), pl.BlockSpec((NB, RB, C), lambda i, *_: (i, 0, 0)), fixed((16, 8, 128))],
            scratch_shapes=[
                pltpu.VMEM((M + 32, C), BF),
                pltpu.VMEM((M + 32, 3 * C), BF),
                pltpu.VMEM((M + 32, C), BF),
                pltpu.VMEM((3, 3 * C, C), BF),
                pltpu.VMEM((3, 3 * C, C), BF),
            ],
        ),
        out_shape=[
            jax.ShapeDtypeStruct((32, 256, C), BF),
            jax.ShapeDtypeStruct((12, RB, C), BF),
            jax.ShapeDtypeStruct((16, 8, 128), jnp.int32),
        ],
        compiler_params=VM,
        cost_estimate=pl.CostEstimate(flops=8 * 10**9, bytes_accessed=12 << 20, transcendentals=0),
        name="front",
    )(tgt, orow, ocol, pre, g2, w2, w1, rows, cols)


def emit_groups(acc, out, lead):
    for g in range(GRP):
        for j in range(9):
            lo = acc[g * 8 : (g + 1) * 8, j * 256 : j * 256 + 128]
            hi = acc[g * 8 : (g + 1) * 8, j * 256 + 128 : (j + 1) * 256]
            out[lead, g, j * 16 : (j + 1) * 16, :] = jnp.concatenate([lo, hi], axis=0).astype(BF)


def terms_kernel(g2_ref, pre_ref, feat_ref, g1_ref, t_ref, vb, vx, x3, acc2, acc1):
    step = pl.program_id(0)

    @pl.when(step == 0)
    def _():
        for b in (vb, vx, x3, acc2, acc1):
            b[...] = jnp.zeros_like(b)

    load_padded(vx, pre_ref, lambda v: jnp.maximum(v, 0))
    spread(x3, vx)
    load_padded(vb, g2_ref)
    gt = vb[pl.ds(16, M), :].T
    for dy in range(3):
        acc2[:, dy * 768 : (dy + 1) * 768] += jnp.dot(gt, x3[pl.ds(dy * 16, M), :], preferred_element_type=F32)
    load_padded(vx, feat_ref)
    spread(x3, vx)
    gt = g1_ref[...].reshape(M, C).T
    for dy in range(3):
        acc1[:, dy * 768 : (dy + 1) * 768] += jnp.dot(gt, x3[pl.ds(dy * 16, M), :], preferred_element_type=F32)

    @pl.when(step == 2)
    def _():
        emit_groups(acc1, t_ref, 0)
        emit_groups(acc2, t_ref, 1)


def terms(g2, pre, feat, g1):
    blk = pl.BlockSpec((NB, 14, 14, C), lambda i: (i, 0, 0, 0))
    return pl.pallas_call(
        terms_kernel,
        grid=(3,),
        in_specs=[blk, blk, blk, pl.BlockSpec((NB, RB, C), lambda i: (i, 0, 0))],
        out_specs=fixed((2, GRP, GR, 128)),
        scratch_shapes=[
            pltpu.VMEM((M + 32, C), BF),
            pltpu.VMEM((M + 32, C), BF),
            pltpu.VMEM((M + 32, 3 * C), BF),
            pltpu.VMEM((C, 9 * C), F32),
            pltpu.VMEM((C, 9 * C), F32),
        ],
        out_shape=jax.ShapeDtypeStruct((2, GRP, GR, 128), BF),
        compiler_params=VM,
        cost_estimate=pl.CostEstimate(flops=8 * 10**9, bytes_accessed=12 << 20, transcendentals=0),
        name="terms",
    )(g2, pre, feat, g1)


def place_kernel(meta, win_ref, own_ref, right_ref, down_ref, diag_ref, canvas):
    canvas[...] = jnp.zeros_like(canvas)

    def slot(s, carry):
        d, k = s // 2, s % 2

        @pl.when(meta[d, 0, 4 * k] == 1)
        def _():
            row, col = meta[d, 0, 4 * k + 1], meta[d, 0, 4 * k + 2]
            for y in range(16):
                w = win_ref[s, y * 16 : (y + 1) * 16, :].astype(F32)
                canvas[0, row + y, pl.ds(col, 16), :] += w[:, 0:128]
                canvas[1, row + y, pl.ds(col, 16), :] += w[:, 128:256]

        return carry

    lax.fori_loop(0, 32, slot, 0)
    for h in range(2):
        part = slice(h * 128, (h + 1) * 128)
        own_ref[:, :, part] = canvas[h, 0:TH, 0:TW, :]
        right_ref[:, :, part] = canvas[h, 0:TH, TW:PW, :].astype(BF)
        down_ref[:, :, part] = canvas[h, TH:, 0:TW, :].astype(BF)
        diag_ref[:, :, part] = canvas[h, TH:, TW:PW, :].astype(BF)


def place(meta, win):
    return pl.pallas_call(
        place_kernel,
        in_specs=[whole(None, pltpu.SMEM), whole(None)],
        out_specs=[whole(None)] * 4,
        out_shape=[
            jax.ShapeDtypeStruct((TH, TW, C), F32),
            jax.ShapeDtypeStruct((TH, 16, C), BF),
            jax.ShapeDtypeStruct((TH, TW, C), BF),
            jax.ShapeDtypeStruct((TH, 16, C), BF),
        ],
        scratch_shapes=[pltpu.VMEM((2, 2 * TH, PW, 128), F32)],
        compiler_params=VM,
        name="place",
    )(meta, win)


def position():
    return lax.axis_index("ty"), lax.axis_index("tx")


def greet(peers):
    barrier = pltpu.get_barrier_semaphore()
    for peer in peers:
        pl.semaphore_signal(barrier, inc=1, device_id=peer, device_id_type=MESH)
    pl.semaphore_wait(barrier, len(peers))


def remote(src, dst, send, recv, peer):
    return pltpu.make_async_remote_copy(src, dst, send, recv, device_id=peer, device_id_type=MESH)


AROUND = [(-1, -1), (-1, 0), (-1, 1), (0, -1), (0, 1), (1, -1), (1, 0), (1, 1)]


def tile_kernel(own, right, down, diag, grad, inp, fg_pad, in_pad, fg, cols_out, rows_in, cols_in, r_right, r_down, r_diag, ssem, rsem):
    ty, tx = position()
    peer = {(a, b): (lax.rem(ty + a + 8, 8), lax.rem(tx + b + 16, 16)) for a, b in AROUND}
    there = {(a, b): jnp.logical_and(
        (ty + a >= 0) & (ty + a < 8), (tx + b >= 0) & (tx + b < 16)) for a, b in AROUND}
    greet([peer[p] for p in AROUND])

    def halo(n, block):
        cols_out[n, 0] = block[:, 0, :]
        cols_out[n, 1] = block[:, TW - 1, :]
        copies = []
        for i, (a, b) in enumerate(AROUND):
            if b == 0:
                src = block.at[0 if a < 0 else TH - 1]
                dst = rows_in.at[n, 1 if a < 0 else 0]
            else:
                src = cols_out.at[n, 0 if b < 0 else 1]
                dst = cols_in.at[n, 7 - i]
            copies.append(remote(src, dst, ssem.at[n * 8 + i], rsem.at[n * 8 + 7 - i], peer[(a, b)]))
        for copy in copies:
            copy.start()
        return copies

    def build(n, block, pad):
        zero = jnp.zeros((16, C), F32)

        def column(a, b):
            i = AROUND.index((a, b))
            return jnp.where(there[(a, b)], cols_in[n, i].astype(F32), 0.0)

        low = [column(-1, -1), column(0, -1), column(1, -1)]
        high = [column(-1, 1), column(0, 1), column(1, 1)]
        at = lax.broadcasted_iota(jnp.int32, (16, C), 0)

        def edge(parts, y):
            v, r = (parts[0], 15) if y < 0 else (parts[2], 0) if y > 15 else (parts[1], y)
            return v[r : r + 1, :]

        for y in range(-2, 17):
            gap = zero
            if y >= -1:
                gap = jnp.where(at == 0, edge(high, y), gap)
            if y <= 15:
                gap = jnp.where(at == 15, edge(low, y + 1), gap)
            pad[pl.ds(16 + (y + 1) * PW + TW, 16), :] = gap.astype(BF)
        for k, a in ((0, -1), (1, 1)):
            row = jnp.where(there[(a, 0)], rows_in[n, k].astype(F32), 0.0).astype(BF)
            pad[pl.ds(16 + (0 if a < 0 else 17) * PW, TW), :] = row
        for y in range(TH):
            pad[pl.ds(16 + (y + 1) * PW, TW), :] = block[y]

    first = halo(0, inp)
    spill = [
        remote(right, r_right, ssem.at[16], rsem.at[16], peer[(0, 1)]),
        remote(down, r_down, ssem.at[17], rsem.at[17], peer[(1, 0)]),
        remote(diag, r_diag, ssem.at[18], rsem.at[18], peer[(1, 1)]),
    ]
    for copy in spill:
        copy.start()
    for copy in first:
        copy.wait()
    build(0, inp, in_pad)
    for copy in spill:
        copy.wait()
    for y in range(TH):
        total = grad[y].astype(F32) + own[y] + jnp.where(there[(-1, 0)], r_down[y].astype(F32), 0.0)
        side = jnp.where(there[(0, -1)], r_right[y].astype(F32), 0.0)
        side += jnp.where(there[(-1, -1)], r_diag[y].astype(F32), 0.0)
        fg[y, 0:16, :] = (total[0:16] + side).astype(BF)
        fg[y, 16:TW, :] = total[16:].astype(BF)
    second = halo(1, fg)
    for copy in second:
        copy.wait()
    build(1, fg, fg_pad)


def tile_exchange(own, right, down, diag, grad, inp):
    return pl.pallas_call(
        tile_kernel,
        in_specs=[whole(None)] * 6,
        out_specs=[whole(None)] * 2,
        out_shape=[jax.ShapeDtypeStruct((FROWS, C), BF)] * 2,
        scratch_shapes=[
            pltpu.VMEM((TH, TW, C), BF),
            pltpu.VMEM((2, 2, TH, C), BF),
            pltpu.VMEM((2, 2, TW, C), BF),
            pltpu.VMEM((2, 8, TH, C), BF),
            pltpu.VMEM((TH, 16, C), BF),
            pltpu.VMEM((TH, TW, C), BF),
            pltpu.VMEM((TH, 16, C), BF),
            pltpu.SemaphoreType.DMA((19,)),
            pltpu.SemaphoreType.DMA((19,)),
        ],
        compiler_params=pltpu.CompilerParams(vmem_limit_bytes=60 << 20, collective_id=1, has_side_effects=True),
        name="tile_exchange",
    )(own, right, down, diag, grad, inp)


def scatter_kernel(nt, with_meta, *refs):
    if with_meta:
        b, meta, out, meta_in, r0, a1, r1, a2, r2, a3, r3, total, ssem, rsem, msend, mrecv, mlocal = refs
    else:
        b, out, r0, a1, r1, a2, r2, a3, r3, total, ssem, rsem = refs
    ty, tx = position()
    x, c, y, z = ty // 2, ty % 2, tx // 4, tx % 4
    other = (x * 2 + 1 - c, tx)
    px = [(lax.rem(x + k, 4) * 2 + c, tx) for k in (1, 2, 3)]
    py = [(ty, lax.rem(y + k, 4) * 4 + z) for k in (1, 2, 3)]
    pz = [(ty, y * 4 + lax.rem(z + k, 4)) for k in (1, 2, 3)]
    row = [(ty, lax.rem(tx + k, 16)) for k in range(1, 16)]
    greet([other] + px + (row if with_meta else py + pz))
    first = remote(b.at[:, :, 1 - c], r0, ssem.at[0], rsem.at[0], other)
    first.start()
    letters = []
    if with_meta:
        for k in range(1, 16):
            letters.append(
                remote(meta.at[lax.rem(tx + k, 16)], meta_in.at[tx], msend.at[k - 1], mrecv.at[k - 1], row[k - 1])
            )
        for letter in letters:
            letter.start()
        keep = pltpu.make_async_copy(meta.at[tx], meta_in.at[tx], mlocal)
        keep.start()
    first.wait()
    for xx in range(4):
        a1[:, xx] = (b[:, xx, c].astype(F32) + r0[:, xx].astype(F32)).astype(BF)
    copies = [
        remote(a1.at[:, lax.rem(x + k, 4)], r1.at[k - 1], ssem.at[k], rsem.at[k], px[k - 1]) for k in (1, 2, 3)
    ]
    for copy in copies:
        copy.start()
    mine = a1[:, x].astype(F32)
    for copy in copies:
        copy.wait()
    a2[...] = (mine + r1[0].astype(F32) + r1[1].astype(F32) + r1[2].astype(F32)).astype(BF)
    copies = [
        remote(a2.at[:, lax.rem(y + k, 4)], r2.at[k - 1], ssem.at[3 + k], rsem.at[3 + k], py[k - 1]) for k in (1, 2, 3)
    ]
    for copy in copies:
        copy.start()
    mine = a2[:, y].astype(F32)
    for copy in copies:
        copy.wait()
    a3[...] = (mine + r2[0].astype(F32) + r2[1].astype(F32) + r2[2].astype(F32)).astype(BF)
    copies = [remote(a3, r3.at[k - 1], ssem.at[6 + k], rsem.at[6 + k], pz[k - 1]) for k in (1, 2, 3)]
    for copy in copies:
        copy.start()
    for copy in copies:
        copy.wait()
    total[...] = a3[...].astype(F32) + r3[0].astype(F32) + r3[1].astype(F32) + r3[2].astype(F32)
    for t in range(nt):
        for bit in range(2):
            out[t, bit * 18 : (bit + 1) * 18, :] = total[t, pl.ds(2 * z + bit, 18, stride=8), :]
    if with_meta:
        for letter in letters:
            letter.wait()
        keep.wait()


def scatter(parts, meta, cid):
    nt = parts.shape[0]
    shaped = parts.reshape(nt, 4, 2, 4, GR, 128)
    out_shape = [jax.ShapeDtypeStruct((nt, 36, 128), F32)]
    scratch = [
        pltpu.VMEM((nt, 4, 4, GR, 128), BF),
        pltpu.VMEM((nt, 4, 4, GR, 128), BF),
        pltpu.VMEM((3, nt, 4, GR, 128), BF),
        pltpu.VMEM((nt, 4, GR, 128), BF),
        pltpu.VMEM((3, nt, GR, 128), BF),
        pltpu.VMEM((nt, GR, 128), BF),
        pltpu.VMEM((3, nt, GR, 128), BF),
        pltpu.VMEM((nt, GR, 128), F32),
        pltpu.SemaphoreType.DMA((10,)),
        pltpu.SemaphoreType.DMA((10,)),
    ]
    operands = [shaped]
    if meta is not None:
        out_shape.append(jax.ShapeDtypeStruct((16, 8, 128), jnp.int32))
        scratch += [pltpu.SemaphoreType.DMA((15,)), pltpu.SemaphoreType.DMA((15,)), pltpu.SemaphoreType.DMA(())]
        operands.append(meta)
    return pl.pallas_call(
        functools.partial(scatter_kernel, nt, meta is not None),
        in_specs=[whole(None)] * len(operands),
        out_specs=[whole(None)] * len(out_shape),
        out_shape=out_shape,
        scratch_shapes=scratch,
        compiler_params=pltpu.CompilerParams(vmem_limit_bytes=60 << 20, collective_id=cid, has_side_effects=True),
        cost_estimate=pl.CostEstimate(flops=10**9, bytes_accessed=16 << 20, transcendentals=0),
        name="scatter",
    )(*operands)


def tile_conv_kernel(fg_pad, in_pad, w_ref, out, t_ref, x3, wt, acc):
    flip_weights(wt, w_ref)
    n = FROWS
    x3[0:16, :] = jnp.zeros((16, 3 * C), BF)
    x3[n - 16 :, :] = jnp.zeros((16, 3 * C), BF)
    spread(x3, fg_pad)
    res = conv_flipped(x3, wt, 16 + PW, FM, PW).astype(BF).reshape(TH, PW, C)
    out[...] = res[:, 0:TW, :]
    at = lax.broadcasted_iota(jnp.int32, (TH, PW, C), 1).reshape(FM, C)
    g = jnp.where(at < TW, fg_pad[pl.ds(16 + PW, FM), :].astype(F32), 0.0).astype(BF)
    gt = g.T
    spread(x3, in_pad)
    for dy in range(3):
        acc[:, dy * 768 : (dy + 1) * 768] = jnp.dot(gt, x3[pl.ds(16 + dy * PW, FM), :], preferred_element_type=F32)
    emit_groups(acc, t_ref, 0)


def tile_conv(fg_pad, in_pad, w):
    return pl.pallas_call(
        tile_conv_kernel,
        in_specs=[whole(None)] * 3,
        out_specs=[whole(None)] * 2,
        out_shape=[jax.ShapeDtypeStruct((TH, TW, C), BF), jax.ShapeDtypeStruct((1, GRP, GR, 128), BF)],
        scratch_shapes=[
            pltpu.VMEM((FROWS, 3 * C), BF),
            pltpu.VMEM((3, 3 * C, C), BF),
            pltpu.VMEM((C, 9 * C), F32),
        ],
        compiler_params=VM,
        name="tile_conv",
    )(fg_pad, in_pad, w)


def local(roi_feat, pre_one, grad_two, w_one, w_two, roi_rows, roi_cols, target_col, off_row, off_col, fpn_input, fpn_grad, w_fpn):
    win, g1, meta = front(target_col[:, 0], off_row, off_col, pre_one, grad_two, w_two, w_one, roi_rows, roi_cols)
    win_in = lax.all_to_all(win.reshape(16, 512, C), "tx", split_axis=0, concat_axis=0, tiled=True)
    parts = terms(grad_two, pre_one, roi_feat, g1)
    heads, meta_in = scatter(parts, meta, 2)
    own, right, down, diag = place(meta_in, win_in.reshape(32, 256, C))
    fg_pad, in_pad = tile_exchange(own, right, down, diag, fpn_grad, fpn_input)
    grad_in, part = tile_conv(fg_pad, in_pad, w_fpn)
    (tail,) = scatter(part, None, 3)
    return grad_in, heads[0].reshape(-1), heads[1].reshape(-1), tail[0].reshape(-1)


def solution(mesh):
    both = ("ty", "tx")
    placed = (
        P(both, None, None, None),
        P(both, None, None, None),
        P(both, None, None, None),
        P(),
        P(),
        P(both, None, None),
        P(both, None, None),
        P(both, None),
        P(both),
        P(both),
        P("ty", "tx", None),
        P("ty", "tx", None),
        P(),
    )
    return jax.shard_map(
        local,
        mesh=mesh,
        in_specs=placed,
        out_specs=(P("ty", "tx", None), P(both), P(both), P(both)),
        check_vma=False,
    )
```

```python
import jax
import jax.numpy as jnp
from jax import lax
from jax.experimental import pallas as pl
from jax.experimental.pallas import tpu as pltpu
from jax.sharding import PartitionSpec as P

F32, BF = jnp.float32, jnp.bfloat16
MESH = pl.DeviceIdType.MESH
C = 256
NB, RB = 4, 240
SR = 200
M = NB * RB
TH, TW, PW = 16, 64, 80
FM = TH * PW
FROWS = 16 + 18 * PW + 16
GR = 144
VM = pltpu.CompilerParams(vmem_limit_bytes=60 << 20)


def whole(shape, space=pltpu.VMEM):
    return pl.BlockSpec(memory_space=space)


def fixed(shape):
    zeros = (0,) * len(shape)
    return pl.BlockSpec(shape, lambda *_: zeros, pipeline_mode=pl.Buffered(1))


def load_padded(dst, src, fn=None, first=0):
    for r in range(NB):
        for y in range(14):
            v = src[first + r, y]
            dst[pl.ds(16 + r * RB + y * 16, 14), :] = v if fn is None else fn(v)


def spread(x3, v):
    n = v.shape[0]
    x3[:, 256:512] = v[...]
    x3[pl.ds(1, n - 1), 0:256] = v[pl.ds(0, n - 1), :]
    x3[pl.ds(0, n - 1), 512:768] = v[pl.ds(1, n - 1), :]


def flip_weights(wt, w):
    for dy in range(3):
        for kk in range(3):
            wt[dy, kk * C : (kk + 1) * C, :] = w[dy, 2 - kk].T


def conv_flipped(x3, wt, base, rows, pitch):
    acc = None
    for dy in range(3):
        t = jnp.dot(x3[pl.ds(base + (1 - dy) * pitch, rows), :], wt[dy], preferred_element_type=F32)
        acc = t if acc is None else acc + t
    return acc


def front_kernel(tgt, orow, ocol, pre_ref, g2_ref, w2_ref, w1_ref, rows_ref, cols_ref, slot_ref, g1_ref, meta_ref, wts_ref, vb, x3, vp, wt2, wt1):
    step = pl.program_id(0)

    @pl.when(step == 0)
    def _():
        vb[...] = jnp.zeros_like(vb)
        vp[...] = jnp.zeros_like(vp)
        x3[0:16] = jnp.zeros((16, 3 * C), BF)
        x3[M + 16 :] = jnp.zeros((16, 3 * C), BF)
        meta_ref[...] = jnp.zeros_like(meta_ref)
        wts_ref[...] = jnp.zeros_like(wts_ref)
        flip_weights(wt2, w2_ref)
        flip_weights(wt1, w1_ref)

    load_padded(vb, g2_ref)
    load_padded(vp, pre_ref)
    spread(x3, vb)
    b2 = conv_flipped(x3, wt2, 16, M, 16)
    g1 = jnp.where(vp[pl.ds(16, M), :] > 0, b2, 0.0).astype(BF)
    g1_ref[...] = g1.reshape(NB, RB, C)
    vb[pl.ds(16, M), :] = g1
    spread(x3, vb)
    rg = conv_flipped(x3, wt1, 16, M, 16).astype(BF)
    lanes = lax.broadcasted_iota(jnp.int32, (8, 128), 1)
    for r in range(NB):
        at = step * NB + r
        t = tgt[at]
        k = lax.fori_loop(0, at, lambda q, s: s + jnp.where(tgt[q] == t, 1, 0), 0)
        for i in range(14):
            slot_ref[t, k, pl.ds(i * 14, 14), :] = rg[r * RB + i * 16 : r * RB + i * 16 + 14]
        old = meta_ref[t]
        new = jnp.where(lanes == 4 * k, 1, old)
        new = jnp.where(lanes == 4 * k + 1, orow[at], new)
        meta_ref[t] = jnp.where(lanes == 4 * k + 2, ocol[at], new)
        wts_ref[t, k, :, 0:14] = rows_ref[r]
        wts_ref[t, k, :, 16:30] = cols_ref[r]


def front(tgt, orow, ocol, pre, g2, w2, w1, rows, cols):
    blk = pl.BlockSpec((NB, 14, 14, C), lambda i, *_: (i, 0, 0, 0))
    rspec = pl.BlockSpec((NB, 16, 14), lambda i, *_: (i, 0, 0))
    return pl.pallas_call(
        front_kernel,
        grid_spec=pltpu.PrefetchScalarGridSpec(
            num_scalar_prefetch=3,
            grid=(3,),
            in_specs=[blk, blk, fixed((3, 3, C, C)), fixed((3, 3, C, C)), rspec, rspec],
            out_specs=[
                fixed((16, 2, SR, C)),
                pl.BlockSpec((NB, RB, C), lambda i, *_: (i, 0, 0)),
                fixed((16, 8, 128)),
                fixed((16, 2, 16, 128)),
            ],
            scratch_shapes=[
                pltpu.VMEM((M + 32, C), BF),
                pltpu.VMEM((M + 32, 3 * C), BF),
                pltpu.VMEM((M + 32, C), BF),
                pltpu.VMEM((3, 3 * C, C), BF),
                pltpu.VMEM((3, 3 * C, C), BF),
            ],
        ),
        out_shape=[
            jax.ShapeDtypeStruct((16, 2, SR, C), BF),
            jax.ShapeDtypeStruct((12, RB, C), BF),
            jax.ShapeDtypeStruct((16, 8, 128), jnp.int32),
            jax.ShapeDtypeStruct((16, 2, 16, 128), BF),
        ],
        compiler_params=VM,
        cost_estimate=pl.CostEstimate(flops=8 * 10**9, bytes_accessed=12 << 20, transcendentals=0),
        name="front",
    )(tgt, orow, ocol, pre, g2, w2, w1, rows, cols)


def emit_groups(value, out, lead):
    for g in range(32):
        for j in range(value.shape[1] // 256):
            lo = value[g * 8 : (g + 1) * 8, j * 256 : j * 256 + 128]
            hi = value[g * 8 : (g + 1) * 8, j * 256 + 128 : (j + 1) * 256]
            both = jnp.concatenate([lo, hi], axis=0).astype(BF)
            out[lead, g // 8, g // 4 % 2, g % 4, j * 16 : (j + 1) * 16, :] = both


def place_kernel(meta, slots, wts, grad, own, p_down, p_right, p_diag, kcol, row0, canvas, rl, cl):
    canvas[...] = jnp.zeros_like(canvas)
    lane = lax.broadcasted_iota(jnp.int32, (128, 256), 1)
    at = lax.broadcasted_iota(jnp.int32, (128, 256), 0)
    i = lane // 14
    j = lane - i * 14
    used = lane < 196
    w = wts[...]
    rl[...] = jnp.dot(w, (used & (i == at)).astype(BF), preferred_element_type=F32).reshape(32, 16, 256)
    cl[...] = jnp.dot(w, (used & (j + 16 == at)).astype(BF), preferred_element_type=F32).reshape(32, 16, 256)
    for h in range(2):
        canvas[h, 0:TH, 0:TW, :] = grad[:, :, h * 128 : (h + 1) * 128].astype(F32)

    def slot(s, carry):
        d, k = s // 2, s % 2

        @pl.when(meta[d, 0, 4 * k] == 1)
        def _():
            row, col = meta[d, 0, 4 * k + 1], meta[d, 0, 4 * k + 2]
            both = (rl[s][:, None, :] * cl[s][None, :, :]).reshape(256, 256).astype(BF)
            win = jnp.dot(both[:, 0:196], slots[d, k, 0:196, :], preferred_element_type=F32)
            for y in range(16):
                for h in range(2):
                    canvas[h, row + y, pl.ds(col, 16), :] += win[y * 16 : (y + 1) * 16, h * 128 : (h + 1) * 128]

        return carry

    lax.fori_loop(0, 32, slot, 0)
    for h in range(2):
        part = slice(h * 128, (h + 1) * 128)
        own[:, :, part] = canvas[h, 0 : TH + 1, 0:TW, :]
        p_down[:, :, part] = canvas[h, TH - 1 : 31, 0:TW, :].astype(BF)
        p_right[:, :, part] = canvas[h, 0 : TH + 1, TW:PW, :].astype(BF)
        p_diag[:, :, part] = canvas[h, TH - 1 : 31, TW:PW, :].astype(BF)
        for n, col in enumerate((0, TW - 1, TW)):
            kcol[n, :, part] = canvas[h, :, col, :].astype(BF)
        row0[:, part] = canvas[h, 0, 0:TW, :].astype(BF)


def place(meta, slots, wts, grad):
    return pl.pallas_call(
        place_kernel,
        in_specs=[whole(None, pltpu.SMEM)] + [whole(None)] * 3,
        out_specs=[whole(None)] * 6,
        out_shape=[
            jax.ShapeDtypeStruct((TH + 1, TW, C), F32),
            jax.ShapeDtypeStruct((TH, TW, C), BF),
            jax.ShapeDtypeStruct((TH + 1, 16, C), BF),
            jax.ShapeDtypeStruct((TH, 16, C), BF),
            jax.ShapeDtypeStruct((3, 32, C), BF),
            jax.ShapeDtypeStruct((TW, C), BF),
        ],
        scratch_shapes=[
            pltpu.VMEM((2, 2 * TH, PW, 128), F32),
            pltpu.VMEM((32, 16, 256), F32),
            pltpu.VMEM((32, 16, 256), F32),
        ],
        compiler_params=VM,
        name="place",
    )(meta, slots, wts, grad)


def position():
    return lax.axis_index("ty"), lax.axis_index("tx")


def greet(peers):
    barrier = pltpu.get_barrier_semaphore()
    for peer in peers:
        pl.semaphore_signal(barrier, inc=1, device_id=peer, device_id_type=MESH)
    pl.semaphore_wait(barrier, len(peers))


def remote(src, dst, send, recv, peer):
    return pltpu.make_async_remote_copy(src, dst, send, recv, device_id=peer, device_id_type=MESH)


def go(copies):
    for copy in copies:
        copy.start()
    return copies


def settle(copies):
    for copy in copies:
        copy.wait()


def summed(mine, got):
    return mine.astype(F32) + got[0].astype(F32) + got[1].astype(F32) + got[2].astype(F32)


AROUND = [(-1, -1), (-1, 0), (-1, 1), (0, -1), (0, 1), (1, -1), (1, 0), (1, 1)]
ROW = [(0, 1), (1, 0), (0, 3), (3, 0), (1, 1), (3, 3), (1, 3), (3, 1), (0, 2), (2, 0), (1, 2), (2, 1), (3, 2), (2, 3), (2, 2)]


def around(ty, tx):
    peer = {(a, b): (lax.rem(ty + a + 8, 8), lax.rem(tx + b + 16, 16)) for a, b in AROUND}
    there = {
        (a, b): (ty + a >= 0) & (ty + a < 8) & (tx + b >= 0) & (tx + b < 16) for a, b in AROUND
    }
    return peer, there


def axes(ty, tx):
    x, c, y, z = ty // 2, ty % 2, tx // 4, tx % 4
    other = (x * 2 + 1 - c, tx)
    px = [(lax.rem(x + k, 4) * 2 + c, tx) for k in (1, 2, 3)]
    py = [(ty, lax.rem(y + k, 4) * 4 + z) for k in (1, 2, 3)]
    pz = [(ty, y * 4 + lax.rem(z + k, 4)) for k in (1, 2, 3)]
    return x, c, y, z, other, px, py, pz


def pad_input(block, pad, rows_in, cols_in, there):
    zero = jnp.zeros((16, C), F32)
    at = lax.broadcasted_iota(jnp.int32, (16, C), 0)

    def column(a, b):
        return jnp.where(there[(a, b)], cols_in[AROUND.index((a, b))].astype(F32), 0.0)

    low = [column(-1, -1), column(0, -1), column(1, -1)]
    high = [column(-1, 1), column(0, 1), column(1, 1)]

    def edge(parts, y):
        v, r = (parts[0], 15) if y < 0 else (parts[2], 0) if y > 15 else (parts[1], y)
        return v[r : r + 1, :]

    for y in range(-2, 17):
        gap = zero
        if y >= -1:
            gap = jnp.where(at == 0, edge(high, y), gap)
        if y <= 15:
            gap = jnp.where(at == 15, edge(low, y + 1), gap)
        pad[pl.ds(16 + (y + 1) * PW + TW, 16), :] = gap.astype(BF)
    pad[FROWS - 16 :, :] = jnp.zeros((16, C), BF)
    for k, a in ((0, -1), (1, 1)):
        row = jnp.where(there[(a, 0)], rows_in[k].astype(F32), 0.0).astype(BF)
        pad[pl.ds(16 + (0 if a < 0 else 17) * PW, TW), :] = row
    for y in range(TH):
        pad[pl.ds(16 + (y + 1) * PW, TW), :] = block[y]


def middle_kernel(
    slots, meta, wts, g2, pre, feat, g1, inp, slots_in, meta_in, wts_in, half, in_pad,
    vg2, vpre, vfeat, vg1, vb, vx, x3, acc2, acc1, parts, r0, a1, r1, cols_out, rows_in, cols_in,
    asend, arecv, msend, mrecv, wsend, wrecv, hsend, hrecv, ssend, srecv, keep, fetch,
):
    ty, tx = position()
    peer, there = around(ty, tx)
    x, c, y, z, other, px, _, _ = axes(ty, tx)
    row = [lax.rem(y + dy, 4) * 4 + lax.rem(z + dz, 4) for dy, dz in ROW]
    loads = go([pltpu.make_async_copy(s, d, fetch.at[i]) for i, (s, d) in enumerate(
        ((pre, vpre), (g2, vg2), (feat, vfeat), (g1, vg1)))])
    cols_out[0] = inp[:, 0, :]
    cols_out[1] = inp[:, TW - 1, :]
    greet([peer[p] for p in AROUND] + [(ty, q) for q in row] + [other] + px)
    letters = go([remote(meta.at[q], meta_in.at[tx], msend.at[i], mrecv.at[i], (ty, q)) for i, q in enumerate(row)])
    letters += go([remote(wts.at[q], wts_in.at[tx], wsend.at[i], wrecv.at[i], (ty, q)) for i, q in enumerate(row)])
    halo = []
    for i, (a, b) in enumerate(AROUND):
        if b == 0:
            src, dst = inp.at[0 if a < 0 else TH - 1], rows_in.at[1 if a < 0 else 0]
        else:
            src, dst = cols_out.at[0 if b < 0 else 1], cols_in.at[7 - i]
        halo.append(remote(src, dst, hsend.at[i], hrecv.at[7 - i], peer[(a, b)]))
    go(halo)
    sent = go([remote(slots.at[q], slots_in.at[tx], asend.at[i], arecv.at[i], (ty, q)) for i, q in enumerate(row)])
    kept = go([
        pltpu.make_async_copy(slots.at[tx], slots_in.at[tx], keep.at[0]),
        pltpu.make_async_copy(meta.at[tx], meta_in.at[tx], keep.at[1]),
        pltpu.make_async_copy(wts.at[tx], wts_in.at[tx], keep.at[2]),
    ])
    for b in (vb, vx, acc2, acc1):
        b[...] = jnp.zeros_like(b)
    x3[0:16] = jnp.zeros((16, 3 * C), BF)
    x3[M + 16 :] = jnp.zeros((16, 3 * C), BF)
    settle(loads)

    def step(n, carry):
        load_padded(vx, vpre, lambda v: jnp.maximum(v, 0), n * NB)
        spread(x3, vx)
        load_padded(vb, vg2, None, n * NB)
        gt = vb[pl.ds(16, M), :].T
        for dy in range(3):
            acc2[:, dy * 768 : (dy + 1) * 768] += jnp.dot(gt, x3[pl.ds(dy * 16, M), :], preferred_element_type=F32)
        load_padded(vx, vfeat, None, n * NB)
        spread(x3, vx)
        gt = vg1[pl.ds(n * NB, NB)].reshape(M, C).T
        for dy in range(3):
            acc1[:, dy * 768 : (dy + 1) * 768] += jnp.dot(gt, x3[pl.ds(dy * 16, M), :], preferred_element_type=F32)
        return carry

    lax.fori_loop(0, 3, step, 0)
    emit_groups(acc1, parts, 0)
    emit_groups(acc2, parts, 1)
    swap = go([remote(parts.at[:, :, 1 - c], r0, ssend.at[0], srecv.at[0], other)])
    settle(halo)
    pad_input(inp, in_pad, rows_in, cols_in, there)
    settle(swap)
    for xx in range(4):
        a1[:, xx] = (parts[:, xx, c].astype(F32) + r0[:, xx].astype(F32)).astype(BF)
    cross = go([remote(a1.at[:, lax.rem(x + k, 4)], r1.at[k - 1], ssend.at[k], srecv.at[k], px[k - 1]) for k in (1, 2, 3)])
    settle(cross)
    half[...] = summed(a1[:, x], r1).astype(BF)
    settle(letters)
    settle(sent)
    settle(kept)


def middle(slots, meta, wts, g2, pre, feat, g1, inp):
    hbm = whole(None, pltpu.HBM)
    vm = whole(None)
    dma = pltpu.SemaphoreType.DMA
    return pl.pallas_call(
        middle_kernel,
        in_specs=[hbm, vm, vm, hbm, hbm, hbm, hbm, vm],
        out_specs=[hbm, vm, vm, vm, vm],
        out_shape=[
            jax.ShapeDtypeStruct((16, 2, SR, C), BF),
            jax.ShapeDtypeStruct((16, 8, 128), jnp.int32),
            jax.ShapeDtypeStruct((16, 2, 16, 128), BF),
            jax.ShapeDtypeStruct((2, 4, GR, 128), BF),
            jax.ShapeDtypeStruct((FROWS, C), BF),
        ],
        scratch_shapes=[
            pltpu.VMEM((12, 14, 14, C), BF),
            pltpu.VMEM((12, 14, 14, C), BF),
            pltpu.VMEM((12, 14, 14, C), BF),
            pltpu.VMEM((12, RB, C), BF),
            pltpu.VMEM((M + 32, C), BF),
            pltpu.VMEM((M + 32, C), BF),
            pltpu.VMEM((M + 32, 3 * C), BF),
            pltpu.VMEM((C, 9 * C), F32),
            pltpu.VMEM((C, 9 * C), F32),
            pltpu.VMEM((2, 4, 2, 4, GR, 128), BF),
            pltpu.VMEM((2, 4, 4, GR, 128), BF),
            pltpu.VMEM((2, 4, 4, GR, 128), BF),
            pltpu.VMEM((3, 2, 4, GR, 128), BF),
            pltpu.VMEM((2, TH, C), BF),
            pltpu.VMEM((2, TW, C), BF),
            pltpu.VMEM((8, TH, C), BF),
            dma((15,)), dma((15,)), dma((15,)), dma((15,)), dma((15,)), dma((15,)),
            dma((8,)), dma((8,)), dma((4,)), dma((4,)), dma((3,)), dma((4,)),
        ],
        compiler_params=pltpu.CompilerParams(vmem_limit_bytes=60 << 20, collective_id=1, has_side_effects=True),
        name="middle",
    )(slots, meta, wts, g2, pre, feat, g1, inp)


ORDER = ("xy", "yx", "xy")


def tail_kernel(
    own, p_down, p_right, p_diag, kcol, row0, in_pad, w_ref, half, out, sums,
    r_down, r_right, r_diag, r_k, r_row0, r_s0, fg_pad, x3i, x3f, wt, parts, r0, a1, ra, a2, rb, a3, rz,
    rh, a3h, rzh, total, tsend, trecv, hsend, hrecv, csend, crecv, dsend, drecv, esend, erecv, zsend, zrecv,
):
    ty, tx = position()
    peer, there = around(ty, tx)
    x, c, y, z, other, px, py, pz = axes(ty, tx)
    greet([peer[p] for p in AROUND] + [other] + px + py + pz)
    tile = [
        remote(p_down, r_down, tsend.at[8], trecv.at[8], peer[(1, 0)]),
        remote(p_right, r_right, tsend.at[9], trecv.at[9], peer[(0, 1)]),
        remote(p_diag, r_diag, tsend.at[10], trecv.at[10], peer[(1, 1)]),
        remote(row0, r_row0, tsend.at[11], trecv.at[11], peer[(-1, 0)]),
        remote(p_right.at[0], r_s0, tsend.at[12], trecv.at[12], peer[(-1, 1)]),
    ]
    for i, (a, b) in enumerate(AROUND):
        src = kcol.at[0 if b < 0 else 1 if b > 0 else 2]
        tile.append(remote(src, r_k.at[7 - i], tsend.at[i], trecv.at[7 - i], peer[(a, b)]))
    go(tile)
    hy = go([remote(half.at[:, lax.rem(y + k, 4)], rh.at[k - 1], hsend.at[k - 1], hrecv.at[k - 1], py[k - 1]) for k in (1, 2, 3)])
    spread(x3i, in_pad)
    fg_pad[FROWS - 16 :, :] = jnp.zeros((16, C), BF)
    flip_weights(wt, w_ref)
    settle(hy)
    a3h[...] = summed(half[:, y], rh).astype(BF)
    hz = go([remote(a3h, rzh.at[k - 1], hsend.at[2 + k], hrecv.at[2 + k], pz[k - 1]) for k in (1, 2, 3)])
    settle(tile)

    up, left, right, below = there[(-1, 0)], there[(0, -1)], there[(0, 1)], there[(1, 0)]
    upleft, belowleft = there[(-1, -1)], there[(1, -1)]
    ks = {p: jnp.where(there[p], r_k[i].astype(F32), 0.0) for i, p in enumerate(AROUND)}
    own_k = kcol[2].astype(F32)
    at = lax.broadcasted_iota(jnp.int32, (16, C), 0)

    def low(v):
        s = jnp.zeros((1, C), F32)
        if 0 <= v:
            s += ks[(0, -1)][v : v + 1]
        if v <= 14:
            s += ks[(-1, -1)][16 + v : 17 + v]
        if v == 16:
            s += ks[(1, -1)][0:1]
        return s if v < 16 else jnp.where(below, s, 0.0)

    def high(v):
        s = jnp.zeros((1, C), F32)
        if 0 <= v:
            s += own_k[v : v + 1] + ks[(0, 1)][v : v + 1]
        if v <= 14:
            s += ks[(-1, 0)][16 + v : 17 + v] + ks[(-1, 1)][16 + v : 17 + v]
        if v == 16:
            s += ks[(1, 0)][0:1] + ks[(1, 1)][0:1]
        s = jnp.where(right, s, 0.0)
        return s if v < 16 else jnp.where(below, s, 0.0)

    for v in range(-2, 17):
        gap = jnp.zeros((16, C), F32)
        if v >= -1:
            gap = jnp.where(at == 0, high(v), gap)
        if v <= 15:
            gap = jnp.where(at == 15, low(v + 1), gap)
        fg_pad[pl.ds(16 + (v + 1) * PW + TW, 16), :] = gap.astype(BF)
    for v in range(-1, 17):
        row = own[v] if v >= 0 else jnp.zeros((TW, C), F32)
        side = jnp.zeros((16, C), F32)
        if v <= 14:
            row = row + jnp.where(up, r_down[v + 1].astype(F32), 0.0)
            side += jnp.where(upleft, r_diag[v + 1].astype(F32), 0.0)
        if v >= 0:
            side += jnp.where(left, r_right[v].astype(F32), 0.0)
        if v == 16:
            row = row + r_row0[...].astype(F32)
            side += jnp.where(belowleft, r_s0[...].astype(F32), 0.0)
        first, rest = row[0:16] + side, row[16:]
        if v == 16:
            first, rest = jnp.where(below, first, 0.0), jnp.where(below, rest, 0.0)
        base = 16 + (v + 1) * PW
        fg_pad[pl.ds(base, 16), :] = first.astype(BF)
        fg_pad[pl.ds(base + 16, TW - 16), :] = rest.astype(BF)

    inside = lax.broadcasted_iota(jnp.int32, (TH, PW, C), 1).reshape(FM, C) < TW
    gt = jnp.where(inside, fg_pad[pl.ds(16 + PW, FM), :].astype(F32), 0.0).astype(BF).T

    def term(q):
        emit_groups(jnp.dot(gt, x3i[pl.ds(16 + q * PW, FM), :], preferred_element_type=F32), parts, q)
        return go([remote(parts.at[q, :, 1 - c], r0.at[q], csend.at[q], crecv.at[q], other)])

    def first_axis(q, swap):
        settle(swap)
        a1[q] = (parts[q, :, c].astype(F32) + r0[q].astype(F32)).astype(BF)
        copies = []
        for k in (1, 2, 3):
            if ORDER[q] == "xy":
                src, to = a1.at[q, lax.rem(x + k, 4)], px[k - 1]
            else:
                src, to = a1.at[q, :, lax.rem(y + k, 4)], py[k - 1]
            copies.append(remote(src, ra.at[q, k - 1], dsend.at[q * 3 + k - 1], drecv.at[q * 3 + k - 1], to))
        return go(copies)

    def second_axis(q, copies):
        mine = a1[q, x] if ORDER[q] == "xy" else a1[q, :, y]
        settle(copies)
        a2[q] = summed(mine, ra[q]).astype(BF)
        copies = []
        for k in (1, 2, 3):
            n, to = (lax.rem(y + k, 4), py[k - 1]) if ORDER[q] == "xy" else (lax.rem(x + k, 4), px[k - 1])
            copies.append(remote(a2.at[q, n], rb.at[q, k - 1], esend.at[q * 3 + k - 1], erecv.at[q * 3 + k - 1], to))
        return go(copies)

    def third_axis(q, copies):
        mine = a2[q, y] if ORDER[q] == "xy" else a2[q, x]
        settle(copies)
        a3[q] = summed(mine, rb[q]).astype(BF)
        return go([remote(a3.at[q], rz.at[q, k - 1], zsend.at[q * 3 + k - 1], zrecv.at[q * 3 + k - 1], pz[k - 1]) for k in (1, 2, 3)])

    def conv(n):
        rows = FM // 2
        res = conv_flipped(x3f, wt, 16 + PW + n * rows, rows, PW).astype(BF).reshape(TH // 2, PW, C)
        out[n * TH // 2 : (n + 1) * TH // 2] = res[:, 0:TW, :]

    s0 = term(0)
    s1 = term(1)
    f0 = first_axis(0, s0)
    s2 = term(2)
    f1 = first_axis(1, s1)
    spread(x3f, fg_pad)
    conv(0)
    f2 = first_axis(2, s2)
    e0 = second_axis(0, f0)
    conv(1)
    e1 = second_axis(1, f1)
    z0 = third_axis(0, e0)
    e2 = second_axis(2, f2)
    z1 = third_axis(1, e1)
    z2 = third_axis(2, e2)
    settle(hz)
    total[0:2] = summed(a3h[...], rzh)
    for q, copies in enumerate((z0, z1, z2)):
        settle(copies)
        total[2, q * 48 : (q + 1) * 48] = summed(a3[q], rz[q])
    for t in range(3):
        for bit in range(2):
            sums[t, bit * 18 : (bit + 1) * 18, :] = total[t, pl.ds(2 * z + bit, 18, stride=8), :]


def tail(own, p_down, p_right, p_diag, kcol, row0, in_pad, w, half):
    vm = whole(None)
    dma = pltpu.SemaphoreType.DMA
    return pl.pallas_call(
        tail_kernel,
        in_specs=[vm] * 9,
        out_specs=[vm] * 2,
        out_shape=[jax.ShapeDtypeStruct((TH, TW, C), BF), jax.ShapeDtypeStruct((3, 36, 128), F32)],
        scratch_shapes=[
            pltpu.VMEM((TH, TW, C), BF),
            pltpu.VMEM((TH + 1, 16, C), BF),
            pltpu.VMEM((TH, 16, C), BF),
            pltpu.VMEM((8, 32, C), BF),
            pltpu.VMEM((TW, C), BF),
            pltpu.VMEM((16, C), BF),
            pltpu.VMEM((FROWS, C), BF),
            pltpu.VMEM((FROWS, 3 * C), BF),
            pltpu.VMEM((FROWS, 3 * C), BF),
            pltpu.VMEM((3, 3 * C, C), BF),
            pltpu.VMEM((3, 4, 2, 4, 48, 128), BF),
            pltpu.VMEM((3, 4, 4, 48, 128), BF),
            pltpu.VMEM((3, 4, 4, 48, 128), BF),
            pltpu.VMEM((3, 3, 4, 48, 128), BF),
            pltpu.VMEM((3, 4, 48, 128), BF),
            pltpu.VMEM((3, 3, 48, 128), BF),
            pltpu.VMEM((3, 48, 128), BF),
            pltpu.VMEM((3, 3, 48, 128), BF),
            pltpu.VMEM((3, 2, GR, 128), BF),
            pltpu.VMEM((2, GR, 128), BF),
            pltpu.VMEM((3, 2, GR, 128), BF),
            pltpu.VMEM((3, GR, 128), F32),
            dma((13,)), dma((13,)), dma((6,)), dma((6,)), dma((3,)), dma((3,)),
            dma((9,)), dma((9,)), dma((9,)), dma((9,)), dma((9,)), dma((9,)),
        ],
        compiler_params=pltpu.CompilerParams(vmem_limit_bytes=60 << 20, collective_id=2, has_side_effects=True),
        name="tail",
    )(own, p_down, p_right, p_diag, kcol, row0, in_pad, w, half)


def local(roi_feat, pre_one, grad_two, w_one, w_two, roi_rows, roi_cols, target_col, off_row, off_col, fpn_input, fpn_grad, w_fpn):
    slots, g1, meta, wts = front(target_col[:, 0], off_row, off_col, pre_one, grad_two, w_two, w_one, roi_rows, roi_cols)
    slots_in, meta_in, wts_in, half, in_pad = middle(slots, meta, wts, grad_two, pre_one, roi_feat, g1, fpn_input)
    own, p_down, p_right, p_diag, kcol, row0 = place(meta_in, slots_in, wts_in.reshape(512, 128), fpn_grad)
    grad_in, sums = tail(own, p_down, p_right, p_diag, kcol, row0, in_pad, w_fpn, half)
    return grad_in, sums[0].reshape(-1), sums[1].reshape(-1), sums[2].reshape(-1)


def solution(mesh):
    both = ("ty", "tx")
    placed = (
        P(both, None, None, None),
        P(both, None, None, None),
        P(both, None, None, None),
        P(),
        P(),
        P(both, None, None),
        P(both, None, None),
        P(both, None),
        P(both),
        P(both),
        P("ty", "tx", None),
        P("ty", "tx", None),
        P(),
    )
    return jax.shard_map(
        local,
        mesh=mesh,
        in_specs=placed,
        out_specs=(P("ty", "tx", None), P(both), P(both), P(both)),
        check_vma=False,
    )
```

```python
import jax
import jax.numpy as jnp
from jax import lax
from jax.experimental import pallas as pl
from jax.experimental.pallas import tpu as pltpu
from jax.sharding import PartitionSpec as P

F32, BF = jnp.float32, jnp.bfloat16
MESH = pl.DeviceIdType.MESH
C = 256
NB, RB = 4, 240
SR = 200
M = NB * RB
TH, TW, PW = 16, 64, 80
FM = TH * PW
FROWS = 16 + 18 * PW + 16
GR = 144
NT = (((1,), (1,)), ((), ()))
VM = pltpu.CompilerParams(vmem_limit_bytes=60 << 20)


def whole(shape, space=pltpu.VMEM):
    return pl.BlockSpec(memory_space=space)


def fixed(shape):
    zeros = (0,) * len(shape)
    return pl.BlockSpec(shape, lambda *_: zeros, pipeline_mode=pl.Buffered(1))


def load_padded(dst, src, fn=None, first=0):
    for r in range(NB):
        for y in range(14):
            v = src[first + r, y]
            dst[pl.ds(16 + r * RB + y * 16, 14), :] = v if fn is None else fn(v)


def spread(x3, v):
    n = v.shape[0]
    x3[:, 256:512] = v[...]
    x3[pl.ds(1, n - 1), 0:256] = v[pl.ds(0, n - 1), :]
    x3[pl.ds(0, n - 1), 512:768] = v[pl.ds(1, n - 1), :]


def line_up(wt, w):
    for dy in range(3):
        for kk in range(3):
            wt[dy, :, kk * C : (kk + 1) * C] = w[dy, 2 - kk]


def conv_flipped(x3, wt, base, rows, pitch):
    acc = None
    for dy in range(3):
        t = lax.dot_general(x3[pl.ds(base + (1 - dy) * pitch, rows), :], wt[dy], NT, preferred_element_type=F32)
        acc = t if acc is None else acc + t
    return acc


def front_kernel(tgt, orow, ocol, pre_ref, g2_ref, w2_ref, w1_ref, rows_ref, cols_ref, slot_ref, g1_ref, meta_ref, wts_ref, vb, x3, vp, wt2, wt1):
    step = pl.program_id(0)

    @pl.when(step == 0)
    def _():
        vb[...] = jnp.zeros_like(vb)
        vp[...] = jnp.zeros_like(vp)
        x3[0:16] = jnp.zeros((16, 3 * C), BF)
        x3[M + 16 :] = jnp.zeros((16, 3 * C), BF)
        meta_ref[...] = jnp.zeros_like(meta_ref)
        wts_ref[...] = jnp.zeros_like(wts_ref)
        slot_ref[...] = jnp.zeros_like(slot_ref)
        line_up(wt2, w2_ref)
        line_up(wt1, w1_ref)

    load_padded(vb, g2_ref)
    load_padded(vp, pre_ref)
    spread(x3, vb)
    b2 = conv_flipped(x3, wt2, 16, M, 16)
    g1 = jnp.where(vp[pl.ds(16, M), :] > 0, b2, 0.0).astype(BF)
    g1_ref[...] = g1.reshape(NB, RB, C)
    vb[pl.ds(16, M), :] = g1
    spread(x3, vb)
    rg = conv_flipped(x3, wt1, 16, M, 16).astype(BF)
    lanes = lax.broadcasted_iota(jnp.int32, (8, 128), 1)
    for r in range(NB):
        at = step * NB + r
        t = tgt[at]
        k = lax.fori_loop(0, at, lambda q, s: s + jnp.where(tgt[q] == t, 1, 0), 0)
        for i in range(14):
            slot_ref[t, k, pl.ds(i * 14, 14), :] = rg[r * RB + i * 16 : r * RB + i * 16 + 14]
        old = meta_ref[t]
        new = jnp.where(lanes == 4 * k, 1, old)
        new = jnp.where(lanes == 4 * k + 1, orow[at], new)
        meta_ref[t] = jnp.where(lanes == 4 * k + 2, ocol[at], new)
        wts_ref[t, k, :, 0:14] = rows_ref[r]
        wts_ref[t, k, :, 16:30] = cols_ref[r]


def front(tgt, orow, ocol, pre, g2, w2, w1, rows, cols):
    blk = pl.BlockSpec((NB, 14, 14, C), lambda i, *_: (i, 0, 0, 0))
    rspec = pl.BlockSpec((NB, 16, 14), lambda i, *_: (i, 0, 0))
    return pl.pallas_call(
        front_kernel,
        grid_spec=pltpu.PrefetchScalarGridSpec(
            num_scalar_prefetch=3,
            grid=(3,),
            in_specs=[blk, blk, fixed((3, 3, C, C)), fixed((3, 3, C, C)), rspec, rspec],
            out_specs=[
                fixed((16, 2, SR, C)),
                pl.BlockSpec((NB, RB, C), lambda i, *_: (i, 0, 0)),
                fixed((16, 8, 128)),
                fixed((16, 2, 16, 128)),
            ],
            scratch_shapes=[
                pltpu.VMEM((M + 32, C), BF),
                pltpu.VMEM((M + 32, 3 * C), BF),
                pltpu.VMEM((M + 32, C), BF),
                pltpu.VMEM((3, C, 3 * C), BF),
                pltpu.VMEM((3, C, 3 * C), BF),
            ],
        ),
        out_shape=[
            jax.ShapeDtypeStruct((16, 2, SR, C), BF),
            jax.ShapeDtypeStruct((12, RB, C), BF),
            jax.ShapeDtypeStruct((16, 8, 128), jnp.int32),
            jax.ShapeDtypeStruct((16, 2, 16, 128), BF),
        ],
        compiler_params=VM,
        cost_estimate=pl.CostEstimate(flops=8 * 10**9, bytes_accessed=12 << 20, transcendentals=0),
        name="front",
    )(tgt, orow, ocol, pre, g2, w2, w1, rows, cols)


def emit_groups(value, out, lead):
    for g in range(32):
        for j in range(value.shape[1] // 256):
            lo = value[g * 8 : (g + 1) * 8, j * 256 : j * 256 + 128]
            hi = value[g * 8 : (g + 1) * 8, j * 256 + 128 : (j + 1) * 256]
            both = jnp.concatenate([lo, hi], axis=0).astype(BF)
            out[lead, g // 8, g // 4 % 2, g % 4, j * 16 : (j + 1) * 16, :] = both


def position():
    return lax.axis_index("ty"), lax.axis_index("tx")


def greet(peers):
    barrier = pltpu.get_barrier_semaphore()
    for peer in peers:
        pl.semaphore_signal(barrier, inc=1, device_id=peer, device_id_type=MESH)
    pl.semaphore_wait(barrier, len(peers))


def remote(src, dst, send, recv, peer):
    return pltpu.make_async_remote_copy(src, dst, send, recv, device_id=peer, device_id_type=MESH)


def go(copies):
    for copy in copies:
        copy.start()
    return copies


def settle(copies):
    for copy in copies:
        copy.wait()


def summed(mine, got):
    return mine.astype(F32) + got[0].astype(F32) + got[1].astype(F32) + got[2].astype(F32)


AROUND = [(-1, -1), (-1, 0), (-1, 1), (0, -1), (0, 1), (1, -1), (1, 0), (1, 1)]
ROW = [(0, 1), (1, 0), (0, 3), (3, 0), (1, 1), (3, 3), (1, 3), (3, 1), (0, 2), (2, 0), (1, 2), (2, 1), (3, 2), (2, 3), (2, 2)]


def around(ty, tx):
    peer = {(a, b): (lax.rem(ty + a + 8, 8), lax.rem(tx + b + 16, 16)) for a, b in AROUND}
    there = {
        (a, b): (ty + a >= 0) & (ty + a < 8) & (tx + b >= 0) & (tx + b < 16) for a, b in AROUND
    }
    return peer, there


def axes(ty, tx):
    x, c, y, z = ty // 2, ty % 2, tx // 4, tx % 4
    other = (x * 2 + 1 - c, tx)
    px = [(lax.rem(x + k, 4) * 2 + c, tx) for k in (1, 2, 3)]
    py = [(ty, lax.rem(y + k, 4) * 4 + z) for k in (1, 2, 3)]
    pz = [(ty, y * 4 + lax.rem(z + k, 4)) for k in (1, 2, 3)]
    return x, c, y, z, other, px, py, pz


def pad_input(block, pad, rows_in, cols_in, there):
    zero = jnp.zeros((16, C), F32)
    at = lax.broadcasted_iota(jnp.int32, (16, C), 0)

    def column(a, b):
        return jnp.where(there[(a, b)], cols_in[AROUND.index((a, b))].astype(F32), 0.0)

    low = [column(-1, -1), column(0, -1), column(1, -1)]
    high = [column(-1, 1), column(0, 1), column(1, 1)]

    def edge(parts, y):
        v, r = (parts[0], 15) if y < 0 else (parts[2], 0) if y > 15 else (parts[1], y)
        return v[r : r + 1, :]

    for y in range(-2, 17):
        gap = zero
        if y >= -1:
            gap = jnp.where(at == 0, edge(high, y), gap)
        if y <= 15:
            gap = jnp.where(at == 15, edge(low, y + 1), gap)
        pad[pl.ds(16 + (y + 1) * PW + TW, 16), :] = gap.astype(BF)
    pad[FROWS - 16 :, :] = jnp.zeros((16, C), BF)
    for k, a in ((0, -1), (1, 1)):
        row = jnp.where(there[(a, 0)], rows_in[k].astype(F32), 0.0).astype(BF)
        pad[pl.ds(16 + (0 if a < 0 else 17) * PW, TW), :] = row
    for y in range(TH):
        pad[pl.ds(16 + (y + 1) * PW, TW), :] = block[y]


ORDER = ("xy", "yx", "xy")
ARRIVALS = ((15, 16), (0, 4), (4, 8), (8, 12), (12, 14), (14, 15))
SCRATCH = {}


def rest_kernel(slots, meta, wts, g2, pre, feat, g1, inp, grad, w, out, sums, *scratch):
    r = dict(zip(SCRATCH, scratch))
    ty, tx = position()
    peer, there = around(ty, tx)
    x, c, y, z, other, px, py, pz = axes(ty, tx)
    row = [(ty, lax.rem(y + dy, 4) * 4 + lax.rem(z + dz, 4)) for dy, dz in ROW]
    pairs = ((inp, "inp"), (pre, "pre"), (g2, "g2"), (feat, "feat"), (g1, "g1"), (grad, "grad"), (w, "w"))
    loads = go([pltpu.make_async_copy(src, r[name], r["fetch"].at[i]) for i, (src, name) in enumerate(pairs)])
    greet([peer[p] for p in AROUND] + row + [other] + px)
    slots_in, meta_in, wts_in = r["slots_in"], r["meta_in"], r["wts_in"]
    tile_in, cols_out = r["inp"], r["cols_out"]
    to = [q[1] for q in row]
    letters = go([remote(meta.at[q], meta_in.at[i], r["msend"].at[i], r["mrecv"].at[i], row[i]) for i, q in enumerate(to)])
    letters += go([remote(wts.at[q], wts_in.at[i], r["wsend"].at[i], r["wrecv"].at[i], row[i]) for i, q in enumerate(to)])
    loads[0].wait()
    cols_out[0] = tile_in[:, 0, :]
    cols_out[1] = tile_in[:, TW - 1, :]
    halo = []
    for i, (a, b) in enumerate(AROUND):
        if b == 0:
            src, dst = tile_in.at[0 if a < 0 else TH - 1], r["rows_in"].at[1 if a < 0 else 0]
        else:
            src, dst = cols_out.at[0 if b < 0 else 1], r["cols_in"].at[7 - i]
        halo.append(remote(src, dst, r["hsend"].at[i], r["hrecv"].at[7 - i], peer[(a, b)]))
    go(halo)
    sent = go([remote(slots.at[q], slots_in.at[i], r["asend"].at[i], r["arecv"].at[i], row[i]) for i, q in enumerate(to)])
    kept = go([
        pltpu.make_async_copy(slots.at[tx], slots_in.at[15], r["keep"].at[0]),
        pltpu.make_async_copy(meta.at[tx], meta_in.at[15], r["keep"].at[1]),
        pltpu.make_async_copy(wts.at[tx], wts_in.at[15], r["keep"].at[2]),
    ])

    vb, vx, x3, acc2, acc1, hparts = r["vb"], r["vx"], r["x3"], r["acc2"], r["acc1"], r["hparts"]
    for buf in (vb, vx, acc2, acc1):
        buf[...] = jnp.zeros_like(buf)
    x3[0:16] = jnp.zeros((16, 3 * C), BF)
    x3[M + 16 :] = jnp.zeros((16, 3 * C), BF)
    settle(loads[1:])

    def step(n, carry):
        load_padded(vx, r["pre"], lambda v: jnp.maximum(v, 0), n * NB)
        spread(x3, vx)
        load_padded(vb, r["g2"], None, n * NB)
        gt = vb[pl.ds(16, M), :].T
        for dy in range(3):
            acc2[:, dy * 768 : (dy + 1) * 768] += jnp.dot(gt, x3[pl.ds(dy * 16, M), :], preferred_element_type=F32)
        load_padded(vx, r["feat"], None, n * NB)
        spread(x3, vx)
        gt = r["g1"][pl.ds(n * NB, NB)].reshape(M, C).T
        for dy in range(3):
            acc1[:, dy * 768 : (dy + 1) * 768] += jnp.dot(gt, x3[pl.ds(dy * 16, M), :], preferred_element_type=F32)
        return carry

    lax.fori_loop(0, 3, step, 0)
    emit_groups(acc1, hparts, 0)
    emit_groups(acc2, hparts, 1)
    swap = go([remote(hparts.at[:, :, 1 - c], r["hr0"], r["ssend"].at[0], r["srecv"].at[0], other)])

    settle(letters)
    settle(kept)
    listed = pltpu.make_async_copy(meta_in, r["smeta"], r["listed"])
    listed.start()
    smeta, canvas, wp, rl, cl = r["smeta"], r["canvas"], r["wp"], r["rl"], r["cl"]
    canvas[...] = jnp.zeros_like(canvas)
    wp[...] = jnp.zeros_like(wp)
    lane = lax.broadcasted_iota(jnp.int32, (128, 256), 1)
    at = lax.broadcasted_iota(jnp.int32, (128, 256), 0)
    bin_row = lane // 14
    bin_col = lane - bin_row * 14
    used = lane < 196
    both_w = wts_in[...].reshape(512, 128)
    rl[...] = jnp.dot(both_w, (used & (bin_row == at)).astype(BF), preferred_element_type=F32).reshape(32, 16, 256)
    cl[...] = jnp.dot(both_w, (used & (bin_col + 16 == at)).astype(BF), preferred_element_type=F32).reshape(32, 16, 256)
    for h in range(2):
        canvas[h, 0:TH, 0:TW, :] = r["grad"][:, :, h * 128 : (h + 1) * 128].astype(F32)
    settle(swap)
    ha1 = r["ha1"]
    for xx in range(4):
        ha1[:, xx] = (hparts[:, xx, c].astype(F32) + r["hr0"][:, xx].astype(F32)).astype(BF)
    cross = go([remote(ha1.at[:, lax.rem(x + k, 4)], r["hr1"].at[k - 1], r["ssend"].at[k], r["srecv"].at[k], px[k - 1]) for k in (1, 2, 3)])
    settle(halo)
    in_pad, x3i, x3f, wt, fg_pad = r["in_pad"], r["x3i"], r["x3f"], r["wt"], r["fg_pad"]
    pad_input(tile_in, in_pad, r["rows_in"], r["cols_in"], there)
    spread(x3i, in_pad)
    line_up(wt, r["w"])
    fg_pad[FROWS - 16 :, :] = jnp.zeros((16, C), BF)
    listed.wait()

    def put(s, carry):
        i, k = s // 2, s % 2
        top = 15 - smeta[i, 0, 4 * k + 1]
        side = TW - smeta[i, 0, 4 * k + 2]
        both = (rl[s][:, None, :] * cl[s][None, :, :]).reshape(256, 256).astype(BF)
        win = jnp.dot(both[:, 0:196], slots_in[i, k, 0:196, :], preferred_element_type=F32)
        for h in range(2):
            wp[h, 15:31, TW : TW + 16, :] = win[:, h * 128 : (h + 1) * 128].reshape(16, 16, 128)
        for v in range(31):
            for h in range(2):
                canvas[h, v] += wp[h, top + v, pl.ds(side, PW), :]
        return carry

    for n, (first, last) in enumerate(ARRIVALS):
        if n:
            for i in range(first, last):
                sent[i].wait_recv()
        lax.fori_loop(2 * first, 2 * last, put, 0)
        if n == 1:
            settle(cross)
            half = r["half"]
            half[...] = summed(ha1[:, x], r["hr1"]).astype(BF)

    p_down, p_right, p_diag, kcol, row0 = r["p_down"], r["p_right"], r["p_diag"], r["kcol"], r["row0"]
    for h in range(2):
        part = slice(h * 128, (h + 1) * 128)
        p_down[:, :, part] = canvas[h, TH - 1 : 31, 0:TW, :].astype(BF)
        p_right[:, :, part] = canvas[h, 0 : TH + 1, TW:PW, :].astype(BF)
        p_diag[:, :, part] = canvas[h, TH - 1 : 31, TW:PW, :].astype(BF)
        for n, col in enumerate((0, TW - 1, TW)):
            kcol[n, :, part] = canvas[h, :, col, :].astype(BF)
        row0[:, part] = canvas[h, 0, 0:TW, :].astype(BF)
    tsend, trecv = r["tsend"], r["trecv"]
    r_down, r_right, r_diag, r_k, r_row0, r_s0 = (r[q] for q in ("r_down", "r_right", "r_diag", "r_k", "r_row0", "r_s0"))
    tile = [
        remote(p_down, r_down, tsend.at[8], trecv.at[8], peer[(1, 0)]),
        remote(p_right, r_right, tsend.at[9], trecv.at[9], peer[(0, 1)]),
        remote(p_diag, r_diag, tsend.at[10], trecv.at[10], peer[(1, 1)]),
        remote(row0, r_row0, tsend.at[11], trecv.at[11], peer[(-1, 0)]),
        remote(p_right.at[0], r_s0, tsend.at[12], trecv.at[12], peer[(-1, 1)]),
    ]
    for i, (a, b) in enumerate(AROUND):
        src = kcol.at[0 if b < 0 else 1 if b > 0 else 2]
        tile.append(remote(src, r_k.at[7 - i], tsend.at[i], trecv.at[7 - i], peer[(a, b)]))
    go(tile)
    hy = go([remote(half.at[:, lax.rem(y + k, 4)], r["rh"].at[k - 1], r["ysend"].at[k - 1], r["yrecv"].at[k - 1], py[k - 1]) for k in (1, 2, 3)])
    for copy in sent:
        copy.wait_send()
    settle(tile)
    parts, r0, a1, ra, a2, rb, a3, rz, rh, a3h, rzh, total, csend, crecv, dsend, drecv, esend, erecv, zsend, zrecv = (
        r[q] for q in (
            "parts", "r0", "a1", "ra", "a2", "rb", "a3", "rz", "rh", "a3h", "rzh", "total", "csend", "crecv", "dsend", "drecv", "esend", "erecv", "zsend", "zrecv",
        )
    )
    up, left, right, below = there[(-1, 0)], there[(0, -1)], there[(0, 1)], there[(1, 0)]
    upleft, belowleft = there[(-1, -1)], there[(1, -1)]
    ks = {p: jnp.where(there[p], r_k[i].astype(F32), 0.0) for i, p in enumerate(AROUND)}
    own_k = kcol[2].astype(F32)
    at = lax.broadcasted_iota(jnp.int32, (16, C), 0)

    def low(v):
        s = jnp.zeros((1, C), F32)
        if 0 <= v:
            s += ks[(0, -1)][v : v + 1]
        if v <= 14:
            s += ks[(-1, -1)][16 + v : 17 + v]
        if v == 16:
            s += ks[(1, -1)][0:1]
        return s if v < 16 else jnp.where(below, s, 0.0)

    def high(v):
        s = jnp.zeros((1, C), F32)
        if 0 <= v:
            s += own_k[v : v + 1] + ks[(0, 1)][v : v + 1]
        if v <= 14:
            s += ks[(-1, 0)][16 + v : 17 + v] + ks[(-1, 1)][16 + v : 17 + v]
        if v == 16:
            s += ks[(1, 0)][0:1] + ks[(1, 1)][0:1]
        s = jnp.where(right, s, 0.0)
        return s if v < 16 else jnp.where(below, s, 0.0)

    for v in range(-2, 17):
        gap = jnp.zeros((16, C), F32)
        if v >= -1:
            gap = jnp.where(at == 0, high(v), gap)
        if v <= 15:
            gap = jnp.where(at == 15, low(v + 1), gap)
        fg_pad[pl.ds(16 + (v + 1) * PW + TW, 16), :] = gap.astype(BF)
    for v in range(-1, 17):
        for h in range(2):
            part = slice(h * 128, (h + 1) * 128)
            line = canvas[h, v, 0:TW, :] if v >= 0 else jnp.zeros((TW, 128), F32)
            side = jnp.zeros((16, 128), F32)
            if v <= 14:
                line = line + jnp.where(up, r_down[v + 1, :, part].astype(F32), 0.0)
                side += jnp.where(upleft, r_diag[v + 1, :, part].astype(F32), 0.0)
            if v >= 0:
                side += jnp.where(left, r_right[v, :, part].astype(F32), 0.0)
            if v == 16:
                line = line + r_row0[:, part].astype(F32)
                side += jnp.where(belowleft, r_s0[:, part].astype(F32), 0.0)
            first, others = line[0:16] + side, line[16:]
            if v == 16:
                first, others = jnp.where(below, first, 0.0), jnp.where(below, others, 0.0)
            base = 16 + (v + 1) * PW
            fg_pad[pl.ds(base, 16), part] = first.astype(BF)
            fg_pad[pl.ds(base + 16, TW - 16), part] = others.astype(BF)

    inside = lax.broadcasted_iota(jnp.int32, (TH, PW, C), 1).reshape(FM, C) < TW
    gt = jnp.where(inside, fg_pad[pl.ds(16 + PW, FM), :].astype(F32), 0.0).astype(BF).T

    def term(q):
        emit_groups(jnp.dot(gt, x3i[pl.ds(16 + q * PW, FM), :], preferred_element_type=F32), parts, q)
        return go([remote(parts.at[q, :, 1 - c], r0.at[q], csend.at[q], crecv.at[q], other)])

    def first_axis(q, swap):
        settle(swap)
        a1[q] = (parts[q, :, c].astype(F32) + r0[q].astype(F32)).astype(BF)
        copies = []
        for k in (1, 2, 3):
            if ORDER[q] == "xy":
                src, to = a1.at[q, lax.rem(x + k, 4)], px[k - 1]
            else:
                src, to = a1.at[q, :, lax.rem(y + k, 4)], py[k - 1]
            copies.append(remote(src, ra.at[q, k - 1], dsend.at[q * 3 + k - 1], drecv.at[q * 3 + k - 1], to))
        return go(copies)

    def second_axis(q, copies):
        mine = a1[q, x] if ORDER[q] == "xy" else a1[q, :, y]
        settle(copies)
        a2[q] = summed(mine, ra[q]).astype(BF)
        copies = []
        for k in (1, 2, 3):
            n, to = (lax.rem(y + k, 4), py[k - 1]) if ORDER[q] == "xy" else (lax.rem(x + k, 4), px[k - 1])
            copies.append(remote(a2.at[q, n], rb.at[q, k - 1], esend.at[q * 3 + k - 1], erecv.at[q * 3 + k - 1], to))
        return go(copies)

    def third_axis(q, copies):
        mine = a2[q, y] if ORDER[q] == "xy" else a2[q, x]
        settle(copies)
        a3[q] = summed(mine, rb[q]).astype(BF)
        return go([remote(a3.at[q], rz.at[q, k - 1], zsend.at[q * 3 + k - 1], zrecv.at[q * 3 + k - 1], pz[k - 1]) for k in (1, 2, 3)])

    def conv(n):
        rows = FM // 2
        res = conv_flipped(x3f, wt, 16 + PW + n * rows, rows, PW).astype(BF).reshape(TH // 2, PW, C)
        out[n * TH // 2 : (n + 1) * TH // 2] = res[:, 0:TW, :]

    settle(hy)
    a3h[...] = summed(half[:, y], rh).astype(BF)
    hz = go([remote(a3h, rzh.at[k - 1], r["ysend"].at[2 + k], r["yrecv"].at[2 + k], pz[k - 1]) for k in (1, 2, 3)])
    s0 = term(0)
    s1 = term(1)
    f0 = first_axis(0, s0)
    s2 = term(2)
    f1 = first_axis(1, s1)
    spread(x3f, fg_pad)
    conv(0)
    f2 = first_axis(2, s2)
    e0 = second_axis(0, f0)
    conv(1)
    e1 = second_axis(1, f1)
    z0 = third_axis(0, e0)
    e2 = second_axis(2, f2)
    z1 = third_axis(1, e1)
    z2 = third_axis(2, e2)
    settle(hz)
    total[0:2] = summed(a3h[...], rzh)
    for q, copies in enumerate((z0, z1, z2)):
        settle(copies)
        total[2, q * 48 : (q + 1) * 48] = summed(a3[q], rz[q])
    for t in range(3):
        for bit in range(2):
            sums[t, bit * 18 : (bit + 1) * 18, :] = total[t, pl.ds(2 * z + bit, 18, stride=8), :]


def rest(slots, meta, wts, g2, pre, feat, g1, inp, grad, w):
    hbm = whole(None, pltpu.HBM)
    vm = whole(None)
    dma = pltpu.SemaphoreType.DMA
    regions = (12, 14, 14, C)
    SCRATCH.clear()
    for name, shape in (
        ("inp", (TH, TW, C)), ("pre", regions), ("g2", regions), ("feat", regions), ("g1", (12, RB, C)),
        ("grad", (TH, TW, C)), ("w", (3, 3, C, C)),
        ("slots_in", (16, 2, SR, C)), ("wts_in", (16, 2, 16, 128)),
        ("vb", (M + 32, C)), ("vx", (M + 32, C)), ("x3", (M + 32, 3 * C)),
        ("hparts", (2, 4, 2, 4, GR, 128)), ("hr0", (2, 4, 4, GR, 128)), ("ha1", (2, 4, 4, GR, 128)),
        ("hr1", (3, 2, 4, GR, 128)), ("half", (2, 4, GR, 128)), ("rh", (3, 2, GR, 128)),
        ("a3h", (2, GR, 128)), ("rzh", (3, 2, GR, 128)),
        ("cols_out", (2, TH, C)), ("rows_in", (2, TW, C)), ("cols_in", (8, TH, C)),
        ("p_down", (TH, TW, C)), ("p_right", (TH + 1, 16, C)), ("p_diag", (TH, 16, C)), ("kcol", (3, 32, C)), ("row0", (TW, C)),
        ("r_down", (TH, TW, C)), ("r_right", (TH + 1, 16, C)), ("r_diag", (TH, 16, C)), ("r_k", (8, 32, C)),
        ("r_row0", (TW, C)), ("r_s0", (16, C)),
        ("in_pad", (FROWS, C)), ("fg_pad", (FROWS, C)), ("x3i", (FROWS, 3 * C)), ("x3f", (FROWS, 3 * C)), ("wt", (3, C, 3 * C)),
        ("parts", (3, 4, 2, 4, 48, 128)), ("r0", (3, 4, 4, 48, 128)), ("a1", (3, 4, 4, 48, 128)), ("ra", (3, 3, 4, 48, 128)),
        ("a2", (3, 4, 48, 128)), ("rb", (3, 3, 48, 128)), ("a3", (3, 48, 128)), ("rz", (3, 3, 48, 128)),
    ):
        SCRATCH[name] = pltpu.VMEM(shape, BF)
    for name, shape in (
        ("acc2", (C, 9 * C)), ("acc1", (C, 9 * C)), ("canvas", (2, 2 * TH, PW, 128)), ("wp", (2, 46, 144, 128)),
        ("rl", (32, 16, 256)), ("cl", (32, 16, 256)), ("total", (3, GR, 128)),
    ):
        SCRATCH[name] = pltpu.VMEM(shape, F32)
    SCRATCH["meta_in"] = pltpu.VMEM((16, 8, 128), jnp.int32)
    SCRATCH["smeta"] = pltpu.SMEM((16, 8, 128), jnp.int32)
    for name, n in (
        ("fetch", 7), ("msend", 15), ("mrecv", 15), ("wsend", 15), ("wrecv", 15), ("asend", 15), ("arecv", 15),
        ("hsend", 8), ("hrecv", 8), ("keep", 3), ("ssend", 4), ("srecv", 4), ("ysend", 6), ("yrecv", 6),
        ("tsend", 13), ("trecv", 13), ("csend", 3), ("crecv", 3), ("dsend", 9), ("drecv", 9), ("esend", 9), ("erecv", 9),
        ("zsend", 9), ("zrecv", 9),
    ):
        SCRATCH[name] = dma((n,))
    SCRATCH["listed"] = dma(())
    return pl.pallas_call(
        rest_kernel,
        in_specs=[hbm, vm, vm] + [hbm] * 7,
        out_specs=[vm] * 2,
        out_shape=[jax.ShapeDtypeStruct((TH, TW, C), BF), jax.ShapeDtypeStruct((3, 36, 128), F32)],
        scratch_shapes=list(SCRATCH.values()),
        compiler_params=pltpu.CompilerParams(vmem_limit_bytes=63 << 20, collective_id=1, has_side_effects=True),
        name="rest",
    )(slots, meta, wts, g2, pre, feat, g1, inp, grad, w)


def local(roi_feat, pre_one, grad_two, w_one, w_two, roi_rows, roi_cols, target_col, off_row, off_col, fpn_input, fpn_grad, w_fpn):
    slots, g1, meta, wts = front(target_col[:, 0], off_row, off_col, pre_one, grad_two, w_two, w_one, roi_rows, roi_cols)
    grad_in, sums = rest(slots, meta, wts, grad_two, pre_one, roi_feat, g1, fpn_input, fpn_grad, w_fpn)
    return grad_in, sums[0].reshape(-1), sums[1].reshape(-1), sums[2].reshape(-1)


def solution(mesh):
    both = ("ty", "tx")
    placed = (
        P(both, None, None, None),
        P(both, None, None, None),
        P(both, None, None, None),
        P(),
        P(),
        P(both, None, None),
        P(both, None, None),
        P(both, None),
        P(both),
        P(both),
        P("ty", "tx", None),
        P("ty", "tx", None),
        P(),
    )
    return jax.shard_map(
        local,
        mesh=mesh,
        in_specs=placed,
        out_specs=(P("ty", "tx", None), P(both), P(both), P(both)),
        check_vma=False,
    )
```

```python
import functools

import jax
import jax.numpy as jnp
from jax import lax
from jax.experimental import pallas as pl
from jax.experimental.pallas import tpu as pltpu
from jax.sharding import PartitionSpec as P

F32, BF = jnp.float32, jnp.bfloat16
MESH = pl.DeviceIdType.MESH
C = 256
NB, RB = 4, 240
SR = 200
M = NB * RB
TH, TW, PW = 16, 64, 80
FM = TH * PW
FROWS = 16 + 18 * PW + 16
GR = 144
NT = (((1,), (1,)), ((), ()))
VM = pltpu.CompilerParams(vmem_limit_bytes=60 << 20)


def whole(shape, space=pltpu.VMEM):
    return pl.BlockSpec(memory_space=space)


def fixed(shape):
    zeros = (0,) * len(shape)
    return pl.BlockSpec(shape, lambda *_: zeros, pipeline_mode=pl.Buffered(1))


def load_padded(dst, src, fn=None, first=0):
    for r in range(NB):
        for y in range(14):
            v = src[first + r, y]
            dst[pl.ds(16 + r * RB + y * 16, 14), :] = v if fn is None else fn(v)


def spread(x3, v):
    n = v.shape[0]
    x3[:, 256:512] = v[...]
    x3[pl.ds(1, n - 1), 0:256] = v[pl.ds(0, n - 1), :]
    x3[pl.ds(0, n - 1), 512:768] = v[pl.ds(1, n - 1), :]


def line_up(wt, w):
    for dy in range(3):
        for kk in range(3):
            wt[dy, :, kk * C : (kk + 1) * C] = w[dy, 2 - kk]


def conv_flipped(x3, wt, base, rows, pitch):
    acc = None
    for dy in range(3):
        t = lax.dot_general(x3[pl.ds(base + (1 - dy) * pitch, rows), :], wt[dy], NT, preferred_element_type=F32)
        acc = t if acc is None else acc + t
    return acc


def emit_groups(value, out, lead):
    for g in range(32):
        for j in range(value.shape[1] // 256):
            lo = value[g * 8 : (g + 1) * 8, j * 256 : j * 256 + 128]
            hi = value[g * 8 : (g + 1) * 8, j * 256 + 128 : (j + 1) * 256]
            both = jnp.concatenate([lo, hi], axis=0).astype(BF)
            out[lead, g // 8, g // 4 % 2, g % 4, j * 16 : (j + 1) * 16, :] = both


def position():
    return lax.axis_index("ty"), lax.axis_index("tx")


def announce(peers):
    barrier = pltpu.get_barrier_semaphore()
    for peer in peers:
        pl.semaphore_signal(barrier, inc=1, device_id=peer, device_id_type=MESH)


def remote(src, dst, send, recv, peer):
    return pltpu.make_async_remote_copy(src, dst, send, recv, device_id=peer, device_id_type=MESH)


def go(copies):
    for copy in copies:
        copy.start()
    return copies


def settle(copies):
    for copy in copies:
        copy.wait()


def summed(mine, got):
    return mine.astype(F32) + got[0].astype(F32) + got[1].astype(F32) + got[2].astype(F32)


AROUND = [(-1, -1), (-1, 0), (-1, 1), (0, -1), (0, 1), (1, -1), (1, 0), (1, 1)]
ROW = [(0, 1), (1, 0), (0, 3), (3, 0), (1, 1), (3, 3), (1, 3), (3, 1), (0, 2), (2, 0), (1, 2), (2, 1), (3, 2), (2, 3), (2, 2)]


def around(ty, tx):
    peer = {(a, b): (lax.rem(ty + a + 8, 8), lax.rem(tx + b + 16, 16)) for a, b in AROUND}
    there = {
        (a, b): (ty + a >= 0) & (ty + a < 8) & (tx + b >= 0) & (tx + b < 16) for a, b in AROUND
    }
    return peer, there


def axes(ty, tx):
    x, c, y, z = ty // 2, ty % 2, tx // 4, tx % 4
    other = (x * 2 + 1 - c, tx)
    px = [(lax.rem(x + k, 4) * 2 + c, tx) for k in (1, 2, 3)]
    py = [(ty, lax.rem(y + k, 4) * 4 + z) for k in (1, 2, 3)]
    pz = [(ty, y * 4 + lax.rem(z + k, 4)) for k in (1, 2, 3)]
    return x, c, y, z, other, px, py, pz


ROWS_FIRST = (False, False, True)
ARRIVALS = ((15, 16), (0, 4), (4, 8), (8, 12), (12, 14), (14, 15))
class Store:
    pass


def all_kernel(names, tgt, orow, ocol, rows, cols, pre, g2, feat, w2, w1, inp, grad, w, out, sums, *scratch):
    r = Store()
    for name, ref in zip(names, scratch):
        setattr(r, name, ref)
    ty, tx = position()
    peer, there = around(ty, tx)
    x, c, y, z, other, px, py, pz = axes(ty, tx)
    row = [(ty, lax.rem(y + dy, 4) * 4 + lax.rem(z + dz, 4)) for dy, dz in ROW]
    to = [q[1] for q in row]
    pairs = (
        (inp, r.inp), (pre, r.pre), (g2, r.g2), (w2, r.w2), (w1, r.w1), (feat, r.feat), (grad, r.grad), (w, r.w),
    )
    loads = go([pltpu.make_async_copy(src, dst, r.fetch.at[i]) for i, (src, dst) in enumerate(pairs)])
    near = [peer[p] for p in AROUND] + row + [other] + px
    announce(near)
    tile_in, col_out = r.inp, r.col_out
    loads[0].wait()
    col_out[...] = tile_in[:, TW - 1, :]
    hsend, hrecv = r.hsend, r.hrecv
    corner = tile_in.at[:, 0:16]
    given = (
        ((-1, -1), corner, r.n_belowright), ((-1, 0), tile_in, r.n_below), ((-1, 1), col_out, r.n_belowleft),
        ((0, -1), corner, r.n_right), ((0, 1), col_out, r.n_left),
        ((1, -1), tile_in.at[TH - 1, 0:16], r.n_upright), ((1, 0), tile_in.at[TH - 1], r.n_up), ((1, 1), col_out, r.n_upleft),
    )

    vb, vx, x3 = r.vb, r.vx, r.x3
    for buf in (vb, vx):
        buf[...] = jnp.zeros_like(buf)
    x3[0:16] = jnp.zeros((16, 3 * C), BF)
    x3[M + 16 :] = jnp.zeros((16, 3 * C), BF)
    rgc, wtl, slotbuf, wtsbuf, metabuf = r.rgc, r.wtl, r.slotbuf, r.wtsbuf, r.metabuf
    rgc[12] = jnp.zeros((SR, C), BF)
    wtl[...] = jnp.zeros_like(wtl)
    for n in range(12):
        wtl[n, :, 0:14] = rows[n]
        wtl[n, :, 16:30] = cols[n]
    settle(loads[1:5])
    line_up(r.wt2, r.w2)
    line_up(r.wt1, r.w1)

    def first(n, carry):
        load_padded(vb, r.g2, None, n * NB)
        load_padded(vx, r.pre, None, n * NB)
        spread(x3, vb)
        b2 = conv_flipped(x3, r.wt2, 16, M, 16)
        g1 = jnp.where(vx[pl.ds(16, M), :] > 0, b2, 0.0).astype(BF)
        r.g1[pl.ds(n * NB, NB)] = g1.reshape(NB, RB, C)
        vb[pl.ds(16, M), :] = g1
        spread(x3, vb)
        rg = conv_flipped(x3, r.wt1, 16, M, 16).astype(BF)
        for q in range(NB):
            for i in range(14):
                rgc[n * NB + q, pl.ds(i * 14, 14), :] = rg[q * RB + i * 16 : q * RB + i * 16 + 14]
        return carry

    first(0, 0)
    pl.semaphore_wait(pltpu.get_barrier_semaphore(), len(near))
    halo = go([remote(src, dst, hsend.at[i], hrecv.at[i], peer[p]) for i, (p, src, dst) in enumerate(given)])
    lax.fori_loop(1, 3, first, 0)
    lanes = lax.broadcasted_iota(jnp.int32, (8, 128), 1)
    targets = [tgt[n] for n in range(12)]
    ranks = []
    for n in range(12):
        rank = jnp.int32(0)
        for q in range(n):
            rank = rank + jnp.where(targets[q] == targets[n], 1, 0)
        ranks.append(targets[n] * 2 + rank)

    def pack(t, carry):
        letter = jnp.zeros((8, 128), jnp.int32)
        for k in range(2):
            n = jnp.int32(12)
            for q in range(12):
                n = jnp.where(ranks[q] == 2 * t + k, q, n)
            m = jnp.minimum(n, 11)
            slotbuf[t, k] = rgc[n]
            wtsbuf[t, k] = wtl[n]
            letter = jnp.where(lanes == 4 * k + 1, jnp.where(n < 12, orow[m], 0), letter)
            letter = jnp.where(lanes == 4 * k + 2, jnp.where(n < 12, ocol[m], 0), letter)
        metabuf[t] = letter
        return carry

    lax.fori_loop(0, 16, pack, 0)
    slots_in, meta_in, wts_in = r.slots_in, r.meta_in, r.wts_in
    letters = go([remote(metabuf.at[q], meta_in.at[i], r.msend.at[i], r.mrecv.at[i], row[i]) for i, q in enumerate(to)])
    letters += go([remote(wtsbuf.at[q], wts_in.at[i], r.wsend.at[i], r.wrecv.at[i], row[i]) for i, q in enumerate(to)])
    sent = go([remote(slotbuf.at[q], slots_in.at[i], r.asend.at[i], r.arecv.at[i], row[i]) for i, q in enumerate(to)])
    kept = go([
        pltpu.make_async_copy(slotbuf.at[tx], slots_in.at[15], r.keep.at[0]),
        pltpu.make_async_copy(metabuf.at[tx], meta_in.at[15], r.keep.at[1]),
        pltpu.make_async_copy(wtsbuf.at[tx], wts_in.at[15], r.keep.at[2]),
    ])

    acc2, acc1, hparts = r.acc2, r.acc1, r.hparts
    for buf in (acc2, acc1):
        buf[...] = jnp.zeros_like(buf)
    settle(loads[5:])

    def step(n, carry):
        load_padded(vx, r.pre, lambda v: jnp.maximum(v, 0), n * NB)
        spread(x3, vx)
        load_padded(vb, r.g2, None, n * NB)
        gt = vb[pl.ds(16, M), :].T
        for dy in range(3):
            acc2[:, dy * 768 : (dy + 1) * 768] += jnp.dot(gt, x3[pl.ds(dy * 16, M), :], preferred_element_type=F32)
        load_padded(vx, r.feat, None, n * NB)
        spread(x3, vx)
        gt = r.g1[pl.ds(n * NB, NB)].reshape(M, C).T
        for dy in range(3):
            acc1[:, dy * 768 : (dy + 1) * 768] += jnp.dot(gt, x3[pl.ds(dy * 16, M), :], preferred_element_type=F32)
        return carry

    lax.fori_loop(0, 3, step, 0)
    emit_groups(acc1, hparts, 0)
    emit_groups(acc2, hparts, 1)
    swap = go([remote(hparts.at[:, :, 1 - c], r.hr0, r.ssend.at[0], r.srecv.at[0], other)])

    settle(letters)
    settle(kept)
    listed = pltpu.make_async_copy(meta_in, r.smeta, r.listed)
    listed.start()
    smeta, canvas, wp, rl, cl = r.smeta, r.canvas, r.wp, r.rl, r.cl
    canvas[...] = jnp.zeros_like(canvas)
    r.by_z[...] = jnp.zeros_like(r.by_z)
    wp[...] = jnp.zeros_like(wp)
    lane = lax.broadcasted_iota(jnp.int32, (128, 256), 1)
    at = lax.broadcasted_iota(jnp.int32, (128, 256), 0)
    bin_row = lane // 14
    bin_col = lane - bin_row * 14
    used = lane < 196
    both_w = wts_in[...].reshape(512, 128)
    rl[...] = jnp.dot(both_w, (used & (bin_row == at)).astype(BF), preferred_element_type=F32).reshape(32, 16, 256)
    cl[...] = jnp.dot(both_w, (used & (bin_col + 16 == at)).astype(BF), preferred_element_type=F32).reshape(32, 16, 256)
    for h in range(2):
        canvas[h, 0:TH, 0:TW, :] = r.grad[:, :, h * 128 : (h + 1) * 128].astype(F32)
    settle(swap)
    ha1 = r.ha1
    for xx in range(4):
        ha1[:, xx] = (hparts[:, xx, c].astype(F32) + r.hr0[:, xx].astype(F32)).astype(BF)
    cross = go([remote(ha1.at[:, lax.rem(x + k, 4)], r.hr1.at[k - 1], r.ssend.at[k], r.srecv.at[k], px[k - 1]) for k in (1, 2, 3)])
    settle(halo)
    strip, x3e, x3f, wt, fg_pad = r.strip, r.x3e, r.x3f, r.wt, r.fg_pad

    def kept_if(p, value):
        return jnp.where(there[p], value.astype(F32), 0.0).astype(BF)

    left_in = [jnp.where(there[p], q[...].astype(F32), 0.0) for p, q in (
        ((-1, -1), r.n_upleft), ((0, -1), r.n_left), ((1, -1), r.n_belowleft))]
    strip[0:16] = jnp.zeros((16, C), BF)
    strip[16 : 16 + TW] = kept_if((-1, 0), r.n_up[...])
    strip[16 + TW : 16 + PW] = kept_if((-1, 1), r.n_upright[...])
    for v in range(TH):
        base = 16 + (v + 1) * PW
        strip[base : base + TW] = tile_in[v]
        strip[base + TW : base + PW] = kept_if((0, 1), r.n_right[v])
        base += TH * PW
        strip[base : base + TW] = kept_if((1, 0), r.n_below[v])
        strip[base + TW : base + PW] = kept_if((1, 1), r.n_belowright[v])
    strip[16 + 33 * PW :] = jnp.zeros((PW + 16, C), BF)
    spread(x3e, strip)
    first_row = lax.broadcasted_iota(jnp.int32, (16, C), 0) == 0
    for v in range(-1, 32):
        edge = left_in[0][15:16] if v < 0 else left_in[1][v : v + 1] if v < TH else left_in[2][v - TH : v - TH + 1]
        base = 16 + (v + 1) * PW
        x3e[base : base + 16, 0:C] = jnp.where(first_row, edge, x3e[base : base + 16, 0:C].astype(F32)).astype(BF)
    line_up(wt, r.w)
    fg_pad[FROWS - 16 :, :] = jnp.zeros((16, C), BF)
    listed.wait()

    def put(s, carry):
        i, k = s // 2, s % 2
        top = 15 - smeta[i, 0, 4 * k + 1]
        side = TW - smeta[i, 0, 4 * k + 2]
        both = (rl[s][:, None, :] * cl[s][None, :, :]).reshape(256, 256).astype(BF)
        win = jnp.dot(both[:, 0:196], slots_in[i, k, 0:196, :], preferred_element_type=F32)
        for h in range(2):
            wp[h, 15:31, TW : TW + 16, :] = win[:, h * 128 : (h + 1) * 128].reshape(16, 16, 128)
        for v in range(31):
            for h in range(2):
                canvas[h, v] += wp[h, top + v, pl.ds(side, PW), :]
        return carry

    for n, (first, last) in enumerate(ARRIVALS):
        if n:
            for i in range(first, last):
                sent[i].wait_recv()
        lax.fori_loop(2 * first, 2 * last, put, 0)
        if n == 1:
            settle(cross)
            half = r.half
            half[...] = summed(ha1[:, x], r.hr1).astype(BF)
            hy = go([remote(half.at[:, lax.rem(y + k, 4)], r.rh.at[k - 1], r.ysend.at[k - 1], r.yrecv.at[k - 1], py[k - 1]) for k in (1, 2, 3)])

    p_down, p_right, p_diag, kcol, row0 = r.p_down, r.p_right, r.p_diag, r.kcol, r.row0
    for h in range(2):
        part = slice(h * 128, (h + 1) * 128)
        p_down[:, :, part] = canvas[h, TH - 1 : 31, 0:TW, :].astype(BF)
        p_right[:, :, part] = canvas[h, 0 : TH + 1, TW:PW, :].astype(BF)
        p_diag[:, :, part] = canvas[h, TH - 1 : 31, TW:PW, :].astype(BF)
        for n, col in enumerate((0, TW - 1, TW)):
            kcol[n, :, part] = canvas[h, :, col, :].astype(BF)
        row0[:, part] = canvas[h, 0, 0:TW, :].astype(BF)
    tsend, trecv = r.tsend, r.trecv
    r_down = r.r_down
    r_right = r.r_right
    r_diag = r.r_diag
    r_k = r.r_k
    r_row0 = r.r_row0
    r_s0 = r.r_s0
    tile = [
        remote(p_down, r_down, tsend.at[8], trecv.at[8], peer[(1, 0)]),
        remote(p_right, r_right, tsend.at[9], trecv.at[9], peer[(0, 1)]),
        remote(p_diag, r_diag, tsend.at[10], trecv.at[10], peer[(1, 1)]),
        remote(row0, r_row0, tsend.at[11], trecv.at[11], peer[(-1, 0)]),
        remote(p_right.at[0], r_s0, tsend.at[12], trecv.at[12], peer[(-1, 1)]),
    ]
    for i, (a, b) in enumerate(AROUND):
        src = kcol.at[0 if b < 0 else 1 if b > 0 else 2]
        tile.append(remote(src, r_k.at[7 - i], tsend.at[i], trecv.at[7 - i], peer[(a, b)]))
    go(tile)
    parts = r.parts
    r0 = r.r0
    a1 = r.a1
    ra = r.ra
    a2 = r.a2
    rb = r.rb
    a3 = r.a3
    rz = r.rz
    rh = r.rh
    a3h = r.a3h
    rzh = r.rzh
    total = r.total
    csend = r.csend
    crecv = r.crecv
    dsend = r.dsend
    drecv = r.drecv
    esend = r.esend
    erecv = r.erecv
    zsend = r.zsend
    zrecv = r.zrecv
    line_at = lax.broadcasted_iota(jnp.int32, (32, PW, 128), 0)
    col_at = lax.broadcasted_iota(jnp.int32, (32, PW, 128), 1)
    inside = ((line_at < TH) | there[(1, 0)]) & ((col_at < TW) | there[(0, 1)])
    for h in range(2):
        part = jnp.where(inside, canvas[h], 0.0).astype(BF).reshape(32 * PW, 128)
        r.whole_t[h * 128 : (h + 1) * 128, :] = part.T
    whole_t = r.whole_t[...]

    def term(q):
        emit_groups(jnp.dot(whole_t, x3e[pl.ds(16 + q * PW, 32 * PW), :], preferred_element_type=F32), parts, q)
        return go([remote(parts.at[q, :, 1 - c], r0.at[q], csend.at[q], crecv.at[q], other)])

    def first_axis(q, swap):
        settle(swap)
        a1[q] = (parts[q, :, c].astype(F32) + r0[q].astype(F32)).astype(BF)
        copies = []
        for k in (1, 2, 3):
            if ROWS_FIRST[q]:
                src, to = a1.at[q, lax.rem(x + k, 4)], px[k - 1]
            else:
                src, to = a1.at[q, :, lax.rem(y + k, 4)], py[k - 1]
            copies.append(remote(src, ra.at[q, k - 1], dsend.at[q * 3 + k - 1], drecv.at[q * 3 + k - 1], to))
        return go(copies)

    def second_axis(q, copies):
        mine = a1[q, x] if ROWS_FIRST[q] else a1[q, :, y]
        settle(copies)
        a2[q] = summed(mine, ra[q]).astype(BF)
        copies = []
        for k in (1, 2, 3):
            n, to = (lax.rem(y + k, 4), py[k - 1]) if ROWS_FIRST[q] else (lax.rem(x + k, 4), px[k - 1])
            copies.append(remote(a2.at[q, n], rb.at[q, k - 1], esend.at[q * 3 + k - 1], erecv.at[q * 3 + k - 1], to))
        return go(copies)

    def third_axis(q, copies):
        mine = a2[q, y] if ROWS_FIRST[q] else a2[q, x]
        settle(copies)
        a3[q] = summed(mine, rb[q]).astype(BF)
        return go([remote(a3.at[q], rz.at[q, k - 1], zsend.at[q * 3 + k - 1], zrecv.at[q * 3 + k - 1], pz[k - 1]) for k in (1, 2, 3)])

    s0 = term(0)
    s1 = term(1)
    settle(hy)
    total[0:2] = summed(half[:, y], rh)
    for t in range(2):
        for to_z in range(4):
            for bit in range(2):
                r.by_z[to_z, t, bit * 24 : bit * 24 + 18, :] = total[t, pl.ds(2 * to_z + bit, 18, stride=8), :]
    a3h[...] = r.by_z[...].astype(BF)
    hz = go([remote(a3h.at[lax.rem(z + k, 4)], rzh.at[k - 1], r.ysend.at[2 + k], r.yrecv.at[2 + k], pz[k - 1]) for k in (1, 2, 3)])
    f0 = first_axis(0, s0)
    s2 = term(2)
    f1 = first_axis(1, s1)
    f2 = first_axis(2, s2)
    settle(tile)

    up, left, right, below = there[(-1, 0)], there[(0, -1)], there[(0, 1)], there[(1, 0)]
    upleft, belowleft = there[(-1, -1)], there[(1, -1)]
    ks = {p: jnp.where(there[p], r_k[i].astype(F32), 0.0) for i, p in enumerate(AROUND)}
    own_k = kcol[2].astype(F32)
    at = lax.broadcasted_iota(jnp.int32, (16, C), 0)

    def low(v):
        s = jnp.zeros((1, C), F32)
        if 0 <= v:
            s += ks[(0, -1)][v : v + 1]
        if v <= 14:
            s += ks[(-1, -1)][16 + v : 17 + v]
        if v == 16:
            s += ks[(1, -1)][0:1]
        return s if v < 16 else jnp.where(below, s, 0.0)

    def high(v):
        s = jnp.zeros((1, C), F32)
        if 0 <= v:
            s += own_k[v : v + 1] + ks[(0, 1)][v : v + 1]
        if v <= 14:
            s += ks[(-1, 0)][16 + v : 17 + v] + ks[(-1, 1)][16 + v : 17 + v]
        if v == 16:
            s += ks[(1, 0)][0:1] + ks[(1, 1)][0:1]
        s = jnp.where(right, s, 0.0)
        return s if v < 16 else jnp.where(below, s, 0.0)

    for v in range(-2, 17):
        gap = jnp.zeros((16, C), F32)
        if v >= -1:
            gap = jnp.where(at == 0, high(v), gap)
        if v <= 15:
            gap = jnp.where(at == 15, low(v + 1), gap)
        fg_pad[pl.ds(16 + (v + 1) * PW + TW, 16), :] = gap.astype(BF)
    for v in range(-1, 17):
        for h in range(2):
            part = slice(h * 128, (h + 1) * 128)
            line = canvas[h, v, 0:TW, :] if v >= 0 else jnp.zeros((TW, 128), F32)
            side = jnp.zeros((16, 128), F32)
            if v <= 14:
                line = line + jnp.where(up, r_down[v + 1, :, part].astype(F32), 0.0)
                side += jnp.where(upleft, r_diag[v + 1, :, part].astype(F32), 0.0)
            if v >= 0:
                side += jnp.where(left, r_right[v, :, part].astype(F32), 0.0)
            if v == 16:
                line = line + r_row0[:, part].astype(F32)
                side += jnp.where(belowleft, r_s0[:, part].astype(F32), 0.0)
            first, others = line[0:16] + side, line[16:]
            if v == 16:
                first, others = jnp.where(below, first, 0.0), jnp.where(below, others, 0.0)
            base = 16 + (v + 1) * PW
            fg_pad[pl.ds(base, 16), part] = first.astype(BF)
            fg_pad[pl.ds(base + 16, TW - 16), part] = others.astype(BF)

    def conv(n):
        rows = FM // 2
        res = conv_flipped(x3f, wt, 16 + PW + n * rows, rows, PW).astype(BF).reshape(TH // 2, PW, C)
        out[n * TH // 2 : (n + 1) * TH // 2] = res[:, 0:TW, :]

    e0 = second_axis(0, f0)
    spread(x3f, fg_pad)
    e1 = second_axis(1, f1)
    conv(0)
    e2 = second_axis(2, f2)
    z0 = third_axis(0, e0)
    z1 = third_axis(1, e1)
    conv(1)
    z2 = third_axis(2, e2)
    for copy in sent:
        copy.wait_send()
    settle(hz)
    heads = summed(a3h[z], rzh)
    for t in range(2):
        for bit in range(2):
            sums[t, bit * 18 : (bit + 1) * 18, :] = heads[t, bit * 24 : bit * 24 + 18, :]
    for q, copies in enumerate((z0, z1, z2)):
        settle(copies)
        total[2, q * 48 : (q + 1) * 48] = summed(a3[q], rz[q])
    for bit in range(2):
        sums[2, bit * 18 : (bit + 1) * 18, :] = total[2, pl.ds(2 * z + bit, 18, stride=8), :]


def run_all(tgt, orow, ocol, rows, cols, pre, g2, feat, w2, w1, inp, grad, w):
    hbm = whole(None, pltpu.HBM)
    vm = whole(None)
    dma = pltpu.SemaphoreType.DMA
    regions = (12, 14, 14, C)
    s = Store()
    s.inp = pltpu.VMEM((TH, TW, C), BF)
    s.pre = pltpu.VMEM(regions, BF)
    s.g2 = pltpu.VMEM(regions, BF)
    s.feat = pltpu.VMEM(regions, BF)
    s.g1 = pltpu.VMEM((12, RB, C), BF)
    s.grad = pltpu.VMEM((TH, TW, C), BF)
    s.w = pltpu.VMEM((3, 3, C, C), BF)
    s.w2 = pltpu.VMEM((3, 3, C, C), BF)
    s.w1 = pltpu.VMEM((3, 3, C, C), BF)
    s.wt2 = pltpu.VMEM((3, C, 3 * C), BF)
    s.wt1 = pltpu.VMEM((3, C, 3 * C), BF)
    s.rgc = pltpu.VMEM((13, SR, C), BF)
    s.wtl = pltpu.VMEM((13, 16, 128), BF)
    s.slotbuf = pltpu.VMEM((16, 2, SR, C), BF)
    s.wtsbuf = pltpu.VMEM((16, 2, 16, 128), BF)
    s.slots_in = pltpu.VMEM((16, 2, SR, C), BF)
    s.wts_in = pltpu.VMEM((16, 2, 16, 128), BF)
    s.vb = pltpu.VMEM((M + 32, C), BF)
    s.vx = pltpu.VMEM((M + 32, C), BF)
    s.x3 = pltpu.VMEM((M + 32, 3 * C), BF)
    s.hparts = pltpu.VMEM((2, 4, 2, 4, GR, 128), BF)
    s.hr0 = pltpu.VMEM((2, 4, 4, GR, 128), BF)
    s.ha1 = pltpu.VMEM((2, 4, 4, GR, 128), BF)
    s.hr1 = pltpu.VMEM((3, 2, 4, GR, 128), BF)
    s.half = pltpu.VMEM((2, 4, GR, 128), BF)
    s.rh = pltpu.VMEM((3, 2, GR, 128), BF)
    s.a3h = pltpu.VMEM((4, 2, 48, 128), BF)
    s.rzh = pltpu.VMEM((3, 2, 48, 128), BF)
    s.col_out = pltpu.VMEM((TH, C), BF)
    s.n_belowright = pltpu.VMEM((TH, 16, C), BF)
    s.n_below = pltpu.VMEM((TH, TW, C), BF)
    s.n_belowleft = pltpu.VMEM((TH, C), BF)
    s.n_right = pltpu.VMEM((TH, 16, C), BF)
    s.n_left = pltpu.VMEM((TH, C), BF)
    s.n_upright = pltpu.VMEM((16, C), BF)
    s.n_up = pltpu.VMEM((TW, C), BF)
    s.n_upleft = pltpu.VMEM((TH, C), BF)
    s.p_down = pltpu.VMEM((TH, TW, C), BF)
    s.p_right = pltpu.VMEM((TH + 1, 16, C), BF)
    s.p_diag = pltpu.VMEM((TH, 16, C), BF)
    s.kcol = pltpu.VMEM((3, 32, C), BF)
    s.row0 = pltpu.VMEM((TW, C), BF)
    s.r_down = pltpu.VMEM((TH, TW, C), BF)
    s.r_right = pltpu.VMEM((TH + 1, 16, C), BF)
    s.r_diag = pltpu.VMEM((TH, 16, C), BF)
    s.r_k = pltpu.VMEM((8, 32, C), BF)
    s.r_row0 = pltpu.VMEM((TW, C), BF)
    s.r_s0 = pltpu.VMEM((16, C), BF)
    s.strip = pltpu.VMEM((32 + 34 * PW, C), BF)
    s.x3e = pltpu.VMEM((32 + 34 * PW, 3 * C), BF)
    s.whole_t = pltpu.VMEM((C, 32 * PW), BF)
    s.fg_pad = pltpu.VMEM((FROWS, C), BF)
    s.x3f = pltpu.VMEM((FROWS, 3 * C), BF)
    s.wt = pltpu.VMEM((3, C, 3 * C), BF)
    s.parts = pltpu.VMEM((3, 4, 2, 4, 48, 128), BF)
    s.r0 = pltpu.VMEM((3, 4, 4, 48, 128), BF)
    s.a1 = pltpu.VMEM((3, 4, 4, 48, 128), BF)
    s.ra = pltpu.VMEM((3, 3, 4, 48, 128), BF)
    s.a2 = pltpu.VMEM((3, 4, 48, 128), BF)
    s.rb = pltpu.VMEM((3, 3, 48, 128), BF)
    s.a3 = pltpu.VMEM((3, 48, 128), BF)
    s.rz = pltpu.VMEM((3, 3, 48, 128), BF)
    s.acc2 = pltpu.VMEM((C, 9 * C), F32)
    s.acc1 = pltpu.VMEM((C, 9 * C), F32)
    s.canvas = pltpu.VMEM((2, 2 * TH, PW, 128), F32)
    s.wp = pltpu.VMEM((2, 46, 144, 128), F32)
    s.rl = pltpu.VMEM((32, 16, 256), F32)
    s.cl = pltpu.VMEM((32, 16, 256), F32)
    s.total = pltpu.VMEM((3, GR, 128), F32)
    s.by_z = pltpu.VMEM((4, 2, 48, 128), F32)
    s.metabuf = pltpu.VMEM((16, 8, 128), jnp.int32)
    s.meta_in = pltpu.VMEM((16, 8, 128), jnp.int32)
    s.smeta = pltpu.SMEM((16, 8, 128), jnp.int32)
    s.fetch = dma((8,))
    s.msend = dma((15,))
    s.mrecv = dma((15,))
    s.wsend = dma((15,))
    s.wrecv = dma((15,))
    s.asend = dma((15,))
    s.arecv = dma((15,))
    s.hsend = dma((8,))
    s.hrecv = dma((8,))
    s.keep = dma((3,))
    s.ssend = dma((4,))
    s.srecv = dma((4,))
    s.ysend = dma((6,))
    s.yrecv = dma((6,))
    s.tsend = dma((13,))
    s.trecv = dma((13,))
    s.csend = dma((3,))
    s.crecv = dma((3,))
    s.dsend = dma((9,))
    s.drecv = dma((9,))
    s.esend = dma((9,))
    s.erecv = dma((9,))
    s.zsend = dma((9,))
    s.zrecv = dma((9,))
    s.listed = dma(())
    return pl.pallas_call(
        functools.partial(all_kernel, list(vars(s))),
        in_specs=[whole(None, pltpu.SMEM)] * 3 + [vm] * 2 + [hbm] * 8,
        out_specs=[vm] * 2,
        out_shape=[jax.ShapeDtypeStruct((TH, TW, C), BF), jax.ShapeDtypeStruct((3, 36, 128), F32)],
        scratch_shapes=list(vars(s).values()),
        compiler_params=pltpu.CompilerParams(vmem_limit_bytes=63 << 20, collective_id=1, has_side_effects=True),
        name="run_all",
    )(tgt, orow, ocol, rows, cols, pre, g2, feat, w2, w1, inp, grad, w)


def local(roi_feat, pre_one, grad_two, w_one, w_two, roi_rows, roi_cols, target_col, off_row, off_col, fpn_input, fpn_grad, w_fpn):
    grad_in, sums = run_all(
        target_col[:, 0], off_row, off_col, roi_rows, roi_cols, pre_one, grad_two, roi_feat, w_two, w_one, fpn_input, fpn_grad, w_fpn
    )
    return grad_in, sums[0].reshape(-1), sums[1].reshape(-1), sums[2].reshape(-1)


def solution(mesh):
    both = ("ty", "tx")
    placed = (
        P(both, None, None, None),
        P(both, None, None, None),
        P(both, None, None, None),
        P(),
        P(),
        P(both, None, None),
        P(both, None, None),
        P(both, None),
        P(both),
        P(both),
        P("ty", "tx", None),
        P("ty", "tx", None),
        P(),
    )
    return jax.shard_map(
        local,
        mesh=mesh,
        in_specs=placed,
        out_specs=(P("ty", "tx", None), P(both), P(both), P(both)),
        check_vma=False,
    )
```

```python
import functools

import jax
import jax.numpy as jnp
from jax import lax
from jax.experimental import pallas as pl
from jax.experimental.pallas import tpu as pltpu
from jax.sharding import PartitionSpec as P

F32, BF = jnp.float32, jnp.bfloat16
MESH = pl.DeviceIdType.MESH
C = 256
LINE = 12 * 16
SPAN = 16 + 16 * LINE + 16
CUT = 4
SA, SB = 14 * CUT, 144
TH, TW, PW = 16, 64, 80
FM = TH * PW
FROWS = 16 + 18 * PW + 16
GR = 144
NT = (((1,), (1,)), ((), ()))
VM = pltpu.CompilerParams(vmem_limit_bytes=60 << 20)


def whole(shape, space=pltpu.VMEM):
    return pl.BlockSpec(memory_space=space)


def fixed(shape):
    zeros = (0,) * len(shape)
    return pl.BlockSpec(shape, lambda *_: zeros, pipeline_mode=pl.Buffered(1))


def load_padded(dst, src):
    for n in range(12):
        for y in range(14):
            dst[pl.ds(16 + (y + 1) * LINE + n * 16, 14), :] = src[n, y]


def spread_rows(x3, v, low, high, fn=None):
    for kk in range(3):
        rows = v[pl.ds(low + kk - 1, high - low), :]
        x3[low:high, kk * C : (kk + 1) * C] = rows if fn is None else fn(rows)


def spread(x3, v):
    n = v.shape[0]
    x3[:, 256:512] = v[...]
    x3[pl.ds(1, n - 1), 0:256] = v[pl.ds(0, n - 1), :]
    x3[pl.ds(0, n - 1), 512:768] = v[pl.ds(1, n - 1), :]


def line_up(wt, w, sems):
    return go([
        pltpu.make_async_copy(w.at[dy, 2 - kk], wt.at[dy, :, kk * C : (kk + 1) * C], sems.at[3 * dy + kk])
        for dy in range(3)
        for kk in range(3)
    ])


def conv_flipped(x3, wt, base, rows, pitch):
    acc = None
    for dy in range(3):
        t = lax.dot_general(x3[pl.ds(base + (1 - dy) * pitch, rows), :], wt[dy], NT, preferred_element_type=F32)
        acc = t if acc is None else acc + t
    return acc


def emit_groups(value, out, lead, base=0):
    for g in range(32):
        for j in range(value.shape[1] // 256):
            lo = value[g * 8 : (g + 1) * 8, j * 256 : j * 256 + 128]
            hi = value[g * 8 : (g + 1) * 8, j * 256 + 128 : (j + 1) * 256]
            both = jnp.concatenate([lo, hi], axis=0).astype(BF)
            out[lead, g // 8, g // 4 % 2, g % 4, base + j * 16 : base + (j + 1) * 16, :] = both


def position():
    return lax.axis_index("ty"), lax.axis_index("tx")


def announce(peers):
    barrier = pltpu.get_barrier_semaphore()
    for peer in peers:
        pl.semaphore_signal(barrier, inc=1, device_id=peer, device_id_type=MESH)


def remote(src, dst, send, recv, peer):
    return pltpu.make_async_remote_copy(src, dst, send, recv, device_id=peer, device_id_type=MESH)


def go(copies):
    for copy in copies:
        copy.start()
    return copies


def settle(copies):
    for copy in copies:
        copy.wait()


def summed(mine, got):
    return mine.astype(F32) + got[0].astype(F32) + got[1].astype(F32) + got[2].astype(F32)


AROUND = [(-1, -1), (-1, 0), (-1, 1), (0, -1), (0, 1), (1, -1), (1, 0), (1, 1)]
ROW = [(0, 1), (1, 0), (0, 3), (3, 0), (1, 1), (3, 3), (1, 3), (3, 1), (0, 2), (2, 0), (1, 2), (2, 1), (3, 2), (2, 3), (2, 2)]


def around(ty, tx):
    peer = {(a, b): (lax.rem(ty + a + 8, 8), lax.rem(tx + b + 16, 16)) for a, b in AROUND}
    there = {
        (a, b): (ty + a >= 0) & (ty + a < 8) & (tx + b >= 0) & (tx + b < 16) for a, b in AROUND
    }
    return peer, there


def axes(ty, tx):
    x, c, y, z = ty // 2, ty % 2, tx // 4, tx % 4
    other = (x * 2 + 1 - c, tx)
    px = [(lax.rem(x + k, 4) * 2 + c, tx) for k in (1, 2, 3)]
    py = [(ty, lax.rem(y + k, 4) * 4 + z) for k in (1, 2, 3)]
    pz = [(ty, y * 4 + lax.rem(z + k, 4)) for k in (1, 2, 3)]
    return x, c, y, z, other, px, py, pz


ROWS_FIRST = (False, False, True)
EARLY = 1
class Store:
    pass


def all_kernel(names, tgt, orow, ocol, rows, cols, pre, g2, feat, w2, w1, inp, grad, w, out, sums, *scratch):
    r = Store()
    for name, ref in zip(names, scratch):
        setattr(r, name, ref)
    ty, tx = position()
    peer, there = around(ty, tx)
    x, c, y, z, other, px, py, pz = axes(ty, tx)
    row = [(ty, lax.rem(y + dy, 4) * 4 + lax.rem(z + dz, 4)) for dy, dz in ROW]
    to = [q[1] for q in row]
    pairs = ((inp, r.inp), (pre, r.pre), (g2, r.g2), (feat, r.feat), (grad, r.grad))
    loads = go([pltpu.make_async_copy(src, dst, r.fetch.at[i]) for i, (src, dst) in enumerate(pairs[:3])])
    taps2 = line_up(r.wt2, w2, r.fetch2)
    taps1 = line_up(r.wt1, w1, r.fetch1)
    loads += go([pltpu.make_async_copy(src, dst, r.fetch.at[3 + i]) for i, (src, dst) in enumerate(pairs[3:])])
    taps = line_up(r.wt, w, r.fetch0)
    near = [peer[p] for p in AROUND] + row + [other] + px
    announce(near)
    tile_in, col_out = r.inp, r.col_out
    loads[0].wait()
    col_out[...] = tile_in[:, TW - 1, :]
    hsend, hrecv = r.hsend, r.hrecv
    corner = tile_in.at[:, 0:16]
    given = (
        ((-1, -1), corner, r.n_belowright), ((-1, 0), tile_in, r.n_below), ((-1, 1), col_out, r.n_belowleft),
        ((0, -1), corner, r.n_right), ((0, 1), col_out, r.n_left),
        ((1, -1), tile_in.at[TH - 1, 0:16], r.n_upright), ((1, 0), tile_in.at[TH - 1], r.n_up), ((1, 1), col_out, r.n_upleft),
    )

    vb, vx, vg, x3, x3g = r.vb, r.vx, r.vg, r.x3, r.x3g
    for buf in (vb, vx, vg):
        buf[...] = jnp.zeros_like(buf)
    rgcs, bufs, wtl, wtsbuf, metabuf = (r.rgc_a, r.rgc_b), (r.buf_a, r.buf_b), r.wtl, r.wtsbuf, r.metabuf
    for rgc in rgcs:
        rgc[12] = jnp.zeros(rgc.shape[1:], BF)
    for n in range(12):
        r.rgc_b[n, SB - 16 : SB, :] = jnp.zeros((16, C), BF)
    wtl[...] = jnp.zeros_like(wtl)
    for n in range(12):
        wtl[n, :, 0:14] = rows[n]
        wtl[n, :, 16:30] = cols[n]
    settle(loads[1:3])
    load_padded(vb, r.g2)
    load_padded(vx, r.pre)
    ends = (16, 16 + 16 * LINE)
    spread_rows(x3, vb, *ends)

    def back(first, count):
        base = 16 + (first + 1) * LINE
        b2 = conv_flipped(x3, r.wt2, base, count * LINE, LINE)
        vg[pl.ds(base, count * LINE), :] = jnp.where(vx[pl.ds(base, count * LINE), :] > 0, b2, 0.0).astype(BF)

    def down(first, count, rgc, start):
        rg = conv_flipped(x3g, r.wt1, 16 + (first + 1) * LINE, count * LINE, LINE).astype(BF)
        for n in range(12):
            for i in range(count):
                rgc[n, pl.ds((first + i - start) * 14, 14), :] = rg[i * LINE + n * 16 : i * LINE + n * 16 + 14]

    targets = [tgt[n] for n in range(12)]
    places = []
    for n in range(12):
        rank = jnp.int32(0)
        for q in range(n):
            rank = rank + jnp.where(targets[q] == targets[n], 1, 0)
        places.append(targets[n] * 2 + rank)

    def region_of(t, k):
        n = jnp.int32(12)
        for q in range(12):
            n = jnp.where(places[q] == 2 * t + k, q, n)
        return n

    def pack_a(t, carry):
        letter = jnp.zeros((8, 128), jnp.int32)
        lanes = lax.broadcasted_iota(jnp.int32, (8, 128), 1)
        for k in range(2):
            n = region_of(t, k)
            m = jnp.minimum(n, 11)
            r.buf_a[t, k] = r.rgc_a[n]
            wtsbuf[t, k] = wtl[n]
            letter = jnp.where(lanes == 4 * k + 1, jnp.where(n < 12, orow[m], 0), letter)
            letter = jnp.where(lanes == 4 * k + 2, jnp.where(n < 12, ocol[m], 0), letter)
        metabuf[t] = letter
        return carry

    def pack_b(t, carry):
        for k in range(2):
            r.buf_b[t, k] = r.rgc_b[region_of(t, k)]
        return carry

    settle(taps2)
    back(0, CUT + 1)
    pl.semaphore_wait(pltpu.get_barrier_semaphore(), len(near))
    halo = go([remote(src, dst, hsend.at[i], hrecv.at[i], peer[p]) for i, (p, src, dst) in enumerate(given)])
    spread_rows(x3g, vg, 16, 16 + (CUT + 2) * LINE)
    settle(taps1)
    down(0, CUT, r.rgc_a, 0)
    lax.fori_loop(0, 16, pack_a, 0)
    meta_in, wts_in = r.meta_in, r.wts_in
    letters = go([remote(metabuf.at[q], meta_in.at[i], r.msend.at[i], r.mrecv.at[i], row[i]) for i, q in enumerate(to)])
    letters += go([remote(wtsbuf.at[q], wts_in.at[i], r.wsend.at[i], r.wrecv.at[i], row[i]) for i, q in enumerate(to)])
    sent = go([remote(r.buf_a.at[q], r.in_a.at[i], r.asend.at[i], r.arecv.at[i], row[i]) for i, q in enumerate(to)])
    back(5, 5)
    back(10, 4)
    spread_rows(x3g, vg, 16 + (CUT + 2) * LINE, 16 + 16 * LINE)
    down(4, 5, r.rgc_b, CUT)
    down(9, 5, r.rgc_b, CUT)
    lax.fori_loop(0, 16, pack_b, 0)
    sent_b = go([remote(r.buf_b.at[q], r.in_b.at[i], r.bsend.at[i], r.brecv.at[i], row[i]) for i, q in enumerate(to)])
    kept = go([
        pltpu.make_async_copy(r.buf_a.at[tx], r.in_a.at[15], r.keep.at[0]),
        pltpu.make_async_copy(r.buf_b.at[tx], r.in_b.at[15], r.keep.at[3]),
        pltpu.make_async_copy(metabuf.at[tx], meta_in.at[15], r.keep.at[1]),
        pltpu.make_async_copy(wtsbuf.at[tx], wts_in.at[15], r.keep.at[2]),
    ])

    hparts, gt = r.hparts, r.gt
    settle(loads[3:])

    def weights(lead, v):
        gt[...] = v[pl.ds(16 + LINE, 14 * LINE), :].T
        for dy in range(3):
            part = jnp.dot(gt[...], x3[pl.ds(16 + dy * LINE, 14 * LINE), :], preferred_element_type=F32)
            emit_groups(part, hparts, lead, dy * 48)

    spread_rows(x3, vx, *ends, lambda v: jnp.maximum(v, 0))
    weights(1, vb)
    load_padded(vx, r.feat)
    spread_rows(x3, vx, *ends)
    weights(0, vg)
    swap = go([remote(hparts.at[:, :, 1 - c], r.hr0, r.ssend.at[0], r.srecv.at[0], other)])

    settle(letters)
    settle(kept)
    listed = pltpu.make_async_copy(meta_in, r.smeta, r.listed)
    listed.start()
    smeta, canvas, wp, rl, cl = r.smeta, r.canvas, r.wp, r.rl, r.cl
    canvas[...] = jnp.zeros_like(canvas)
    r.by_z[...] = jnp.zeros_like(r.by_z)
    wp[...] = jnp.zeros_like(wp)
    lane = lax.broadcasted_iota(jnp.int32, (128, 256), 1)
    at = lax.broadcasted_iota(jnp.int32, (128, 256), 0)
    bin_at = jnp.where(lane < 64, lane, lane - 8)
    bin_row = bin_at // 14
    bin_col = bin_at - bin_row * 14
    used = (lane < SA) | ((lane >= 64) & (lane < 204))
    gbuf = r.gbuf
    gbuf[...] = jnp.zeros_like(gbuf)
    both_w = wts_in[...].reshape(512, 128)
    rl[...] = jnp.dot(both_w, (used & (bin_row == at)).astype(BF), preferred_element_type=F32).reshape(32, 16, 256)
    cl[...] = jnp.dot(both_w, (used & (bin_col + 16 == at)).astype(BF), preferred_element_type=F32).reshape(32, 16, 256)
    for h in range(2):
        canvas[h, 0:TH, 0:TW, :] = r.grad[:, :, h * 128 : (h + 1) * 128].astype(F32)
    settle(swap)
    ha1 = r.ha1
    for xx in range(4):
        ha1[:, xx] = (hparts[:, xx, c].astype(F32) + r.hr0[:, xx].astype(F32)).astype(BF)
    cross = go([remote(ha1.at[:, lax.rem(x + k, 4)], r.hr1.at[k - 1], r.ssend.at[k], r.srecv.at[k], px[k - 1]) for k in (1, 2, 3)])
    settle(halo)
    strip, x3e, x3f, wt, fg_pad = vx, x3g, r.x3f, r.wt, r.fg_pad

    def kept_if(p, value):
        return jnp.where(there[p], value.astype(F32), 0.0).astype(BF)

    left_in = [jnp.where(there[p], q[...].astype(F32), 0.0) for p, q in (
        ((-1, -1), r.n_upleft), ((0, -1), r.n_left), ((1, -1), r.n_belowleft))]
    strip[0:16] = jnp.zeros((16, C), BF)
    strip[16 : 16 + TW] = kept_if((-1, 0), r.n_up[...])
    strip[16 + TW : 16 + PW] = kept_if((-1, 1), r.n_upright[...])
    for v in range(TH):
        base = 16 + (v + 1) * PW
        strip[base : base + TW] = tile_in[v]
        strip[base + TW : base + PW] = kept_if((0, 1), r.n_right[v])
        base += TH * PW
        strip[base : base + TW] = kept_if((1, 0), r.n_below[v])
        strip[base + TW : base + PW] = kept_if((1, 1), r.n_belowright[v])
    strip[16 + 33 * PW : 32 + 34 * PW] = jnp.zeros((PW + 16, C), BF)
    spread_rows(x3e, strip, 16, 16 + 34 * PW)
    first_row = lax.broadcasted_iota(jnp.int32, (16, C), 0) == 0
    for v in range(-1, 32):
        edge = left_in[0][15:16] if v < 0 else left_in[1][v : v + 1] if v < TH else left_in[2][v - TH : v - TH + 1]
        base = 16 + (v + 1) * PW
        x3e[base : base + 16, 0:C] = jnp.where(first_row, edge, x3e[base : base + 16, 0:C].astype(F32)).astype(BF)
    settle(taps)
    fg_pad[FROWS - 16 :, :] = jnp.zeros((16, C), BF)
    listed.wait()

    def put(s, carry):
        i, k = s // 2, s % 2
        top = 15 - smeta[i, 0, 4 * k + 1]
        side = TW - smeta[i, 0, 4 * k + 2]
        both = (rl[s][:, None, :] * cl[s][None, :, :]).reshape(256, 256).astype(BF)
        gbuf[0:SA, :] = r.in_a[i, k]
        gbuf[64 : 64 + SB, :] = r.in_b[i, k]
        win = jnp.dot(both, gbuf[...], preferred_element_type=F32)
        for h in range(2):
            wp[h, 15:31, TW : TW + 16, :] = win[:, h * 128 : (h + 1) * 128].reshape(16, 16, 128)
        for v in range(31):
            for h in range(2):
                canvas[h, v] += wp[h, top + v, pl.ds(side, PW), :]
        return carry

    def pair(i, carry):
        remote(r.buf_a.at[0], r.in_a.at[i], r.asend.at[i], r.arecv.at[i], row[0]).wait_recv()
        remote(r.buf_b.at[0], r.in_b.at[i], r.bsend.at[i], r.brecv.at[i], row[0]).wait_recv()
        put(2 * i, 0)
        put(2 * i + 1, 0)
        return carry

    lax.fori_loop(30, 32, put, 0)
    lax.fori_loop(0, EARLY, pair, 0)
    settle(cross)
    half = r.half
    half[...] = summed(ha1[:, x], r.hr1).astype(BF)
    hy = go([remote(half.at[:, lax.rem(y + k, 4)], r.rh.at[k - 1], r.ysend.at[k - 1], r.yrecv.at[k - 1], py[k - 1]) for k in (1, 2, 3)])
    lax.fori_loop(EARLY, 15, pair, 0)

    p_down, p_right, p_diag, kcol, row0 = r.p_down, r.p_right, r.p_diag, r.kcol, r.row0
    for h in range(2):
        part = slice(h * 128, (h + 1) * 128)
        p_down[:, :, part] = canvas[h, TH - 1 : 31, 0:TW, :].astype(BF)
        p_right[:, :, part] = canvas[h, 0 : TH + 1, TW:PW, :].astype(BF)
        p_diag[:, :, part] = canvas[h, TH - 1 : 31, TW:PW, :].astype(BF)
        for n, col in enumerate((0, TW - 1, TW)):
            kcol[n, :, part] = canvas[h, :, col, :].astype(BF)
        row0[:, part] = canvas[h, 0, 0:TW, :].astype(BF)
    tsend, trecv = r.tsend, r.trecv
    r_down = r.r_down
    r_right = r.r_right
    r_diag = r.r_diag
    r_k = r.r_k
    r_row0 = r.r_row0
    r_s0 = r.r_s0
    tile = [
        remote(p_down, r_down, tsend.at[8], trecv.at[8], peer[(1, 0)]),
        remote(p_right, r_right, tsend.at[9], trecv.at[9], peer[(0, 1)]),
        remote(p_diag, r_diag, tsend.at[10], trecv.at[10], peer[(1, 1)]),
        remote(row0, r_row0, tsend.at[11], trecv.at[11], peer[(-1, 0)]),
        remote(p_right.at[0], r_s0, tsend.at[12], trecv.at[12], peer[(-1, 1)]),
    ]
    for i, (a, b) in enumerate(AROUND):
        src = kcol.at[0 if b < 0 else 1 if b > 0 else 2]
        tile.append(remote(src, r_k.at[7 - i], tsend.at[i], trecv.at[7 - i], peer[(a, b)]))
    go(tile)
    parts = r.parts
    r0 = r.r0
    a1 = r.a1
    ra = r.ra
    a2 = r.a2
    rb = r.rb
    a3 = r.a3
    rz = r.rz
    rh = r.rh
    a3h = r.a3h
    rzh = r.rzh
    total = r.total
    csend = r.csend
    crecv = r.crecv
    dsend = r.dsend
    drecv = r.drecv
    esend = r.esend
    erecv = r.erecv
    zsend = r.zsend
    zrecv = r.zrecv
    line_at = lax.broadcasted_iota(jnp.int32, (32, PW, 128), 0)
    col_at = lax.broadcasted_iota(jnp.int32, (32, PW, 128), 1)
    inside = ((line_at < TH) | there[(1, 0)]) & ((col_at < TW) | there[(0, 1)])
    for h in range(2):
        part = jnp.where(inside, canvas[h], 0.0).astype(BF).reshape(32 * PW, 128)
        r.whole_t[h * 128 : (h + 1) * 128, :] = part.T
    whole_t = r.whole_t[...]

    def term(q):
        emit_groups(jnp.dot(whole_t, x3e[pl.ds(16 + q * PW, 32 * PW), :], preferred_element_type=F32), parts, q)
        return go([remote(parts.at[q, :, 1 - c], r0.at[q], csend.at[q], crecv.at[q], other)])

    def first_axis(q, swap):
        settle(swap)
        a1[q] = (parts[q, :, c].astype(F32) + r0[q].astype(F32)).astype(BF)
        copies = []
        for k in (1, 2, 3):
            if ROWS_FIRST[q]:
                src, to = a1.at[q, lax.rem(x + k, 4)], px[k - 1]
            else:
                src, to = a1.at[q, :, lax.rem(y + k, 4)], py[k - 1]
            copies.append(remote(src, ra.at[q, k - 1], dsend.at[q * 3 + k - 1], drecv.at[q * 3 + k - 1], to))
        return go(copies)

    def second_axis(q, copies):
        mine = a1[q, x] if ROWS_FIRST[q] else a1[q, :, y]
        settle(copies)
        a2[q] = summed(mine, ra[q]).astype(BF)
        copies = []
        for k in (1, 2, 3):
            n, to = (lax.rem(y + k, 4), py[k - 1]) if ROWS_FIRST[q] else (lax.rem(x + k, 4), px[k - 1])
            copies.append(remote(a2.at[q, n], rb.at[q, k - 1], esend.at[q * 3 + k - 1], erecv.at[q * 3 + k - 1], to))
        return go(copies)

    def third_axis(q, copies):
        mine = a2[q, y] if ROWS_FIRST[q] else a2[q, x]
        settle(copies)
        a3[q] = summed(mine, rb[q]).astype(BF)
        return go([remote(a3.at[q], rz.at[q, k - 1], zsend.at[q * 3 + k - 1], zrecv.at[q * 3 + k - 1], pz[k - 1]) for k in (1, 2, 3)])

    s0 = term(0)
    s1 = term(1)
    settle(hy)
    total[0:2] = summed(half[:, y], rh)
    for t in range(2):
        for to_z in range(4):
            for bit in range(2):
                r.by_z[to_z, t, bit * 24 : bit * 24 + 18, :] = total[t, pl.ds(2 * to_z + bit, 18, stride=8), :]
    a3h[...] = r.by_z[...].astype(BF)
    hz = go([remote(a3h.at[lax.rem(z + k, 4)], rzh.at[k - 1], r.ysend.at[2 + k], r.yrecv.at[2 + k], pz[k - 1]) for k in (1, 2, 3)])
    f0 = first_axis(0, s0)
    s2 = term(2)
    f1 = first_axis(1, s1)
    f2 = first_axis(2, s2)
    settle(tile)

    up, left, right, below = there[(-1, 0)], there[(0, -1)], there[(0, 1)], there[(1, 0)]
    upleft, belowleft = there[(-1, -1)], there[(1, -1)]
    ks = {p: jnp.where(there[p], r_k[i].astype(F32), 0.0) for i, p in enumerate(AROUND)}
    own_k = kcol[2].astype(F32)
    at = lax.broadcasted_iota(jnp.int32, (16, C), 0)

    def low(v):
        s = jnp.zeros((1, C), F32)
        if 0 <= v:
            s += ks[(0, -1)][v : v + 1]
        if v <= 14:
            s += ks[(-1, -1)][16 + v : 17 + v]
        if v == 16:
            s += ks[(1, -1)][0:1]
        return s if v < 16 else jnp.where(below, s, 0.0)

    def high(v):
        s = jnp.zeros((1, C), F32)
        if 0 <= v:
            s += own_k[v : v + 1] + ks[(0, 1)][v : v + 1]
        if v <= 14:
            s += ks[(-1, 0)][16 + v : 17 + v] + ks[(-1, 1)][16 + v : 17 + v]
        if v == 16:
            s += ks[(1, 0)][0:1] + ks[(1, 1)][0:1]
        s = jnp.where(right, s, 0.0)
        return s if v < 16 else jnp.where(below, s, 0.0)

    for v in range(-2, 17):
        gap = jnp.zeros((16, C), F32)
        if v >= -1:
            gap = jnp.where(at == 0, high(v), gap)
        if v <= 15:
            gap = jnp.where(at == 15, low(v + 1), gap)
        fg_pad[pl.ds(16 + (v + 1) * PW + TW, 16), :] = gap.astype(BF)
    for v in range(-1, 17):
        for h in range(2):
            part = slice(h * 128, (h + 1) * 128)
            line = canvas[h, v, 0:TW, :] if v >= 0 else jnp.zeros((TW, 128), F32)
            side = jnp.zeros((16, 128), F32)
            if v <= 14:
                line = line + jnp.where(up, r_down[v + 1, :, part].astype(F32), 0.0)
                side += jnp.where(upleft, r_diag[v + 1, :, part].astype(F32), 0.0)
            if v >= 0:
                side += jnp.where(left, r_right[v, :, part].astype(F32), 0.0)
            if v == 16:
                line = line + r_row0[:, part].astype(F32)
                side += jnp.where(belowleft, r_s0[:, part].astype(F32), 0.0)
            first, others = line[0:16] + side, line[16:]
            if v == 16:
                first, others = jnp.where(below, first, 0.0), jnp.where(below, others, 0.0)
            base = 16 + (v + 1) * PW
            fg_pad[pl.ds(base, 16), part] = first.astype(BF)
            fg_pad[pl.ds(base + 16, TW - 16), part] = others.astype(BF)

    def conv(n):
        rows = FM // 2
        res = conv_flipped(x3f, wt, 16 + PW + n * rows, rows, PW).astype(BF).reshape(TH // 2, PW, C)
        out[n * TH // 2 : (n + 1) * TH // 2] = res[:, 0:TW, :]

    e0 = second_axis(0, f0)
    spread(x3f, fg_pad)
    e1 = second_axis(1, f1)
    conv(0)
    e2 = second_axis(2, f2)
    z0 = third_axis(0, e0)
    z1 = third_axis(1, e1)
    conv(1)
    z2 = third_axis(2, e2)
    for copy in sent + sent_b:
        copy.wait_send()
    settle(hz)
    heads = summed(a3h[z], rzh)
    for t in range(2):
        for bit in range(2):
            sums[t, bit * 18 : (bit + 1) * 18, :] = heads[t, bit * 24 : bit * 24 + 18, :]
    for q, copies in enumerate((z0, z1, z2)):
        settle(copies)
        total[2, q * 48 : (q + 1) * 48] = summed(a3[q], rz[q])
    for bit in range(2):
        sums[2, bit * 18 : (bit + 1) * 18, :] = total[2, pl.ds(2 * z + bit, 18, stride=8), :]


def run_all(tgt, orow, ocol, rows, cols, pre, g2, feat, w2, w1, inp, grad, w):
    hbm = whole(None, pltpu.HBM)
    vm = whole(None)
    dma = pltpu.SemaphoreType.DMA
    regions = (12, 14, 14, C)
    s = Store()
    s.inp = pltpu.VMEM((TH, TW, C), BF)
    s.pre = pltpu.VMEM(regions, BF)
    s.g2 = pltpu.VMEM(regions, BF)
    s.feat = pltpu.VMEM(regions, BF)
    s.grad = pltpu.VMEM((TH, TW, C), BF)
    s.wt2 = pltpu.VMEM((3, C, 3 * C), BF)
    s.wt1 = pltpu.VMEM((3, C, 3 * C), BF)
    s.wtl = pltpu.VMEM((13, 16, 128), BF)
    s.wtsbuf = pltpu.VMEM((16, 2, 16, 128), BF)
    s.wts_in = pltpu.VMEM((16, 2, 16, 128), BF)
    s.hparts = pltpu.VMEM((2, 4, 2, 4, GR, 128), BF)
    s.hr0 = pltpu.VMEM((2, 4, 4, GR, 128), BF)
    s.ha1 = pltpu.VMEM((2, 4, 4, GR, 128), BF)
    s.hr1 = pltpu.VMEM((3, 2, 4, GR, 128), BF)
    s.half = pltpu.VMEM((2, 4, GR, 128), BF)
    s.rh = pltpu.VMEM((3, 2, GR, 128), BF)
    s.a3h = pltpu.VMEM((4, 2, 48, 128), BF)
    s.rzh = pltpu.VMEM((3, 2, 48, 128), BF)
    s.col_out = pltpu.VMEM((TH, C), BF)
    s.n_belowright = pltpu.VMEM((TH, 16, C), BF)
    s.n_below = pltpu.VMEM((TH, TW, C), BF)
    s.n_belowleft = pltpu.VMEM((TH, C), BF)
    s.n_right = pltpu.VMEM((TH, 16, C), BF)
    s.n_left = pltpu.VMEM((TH, C), BF)
    s.n_upright = pltpu.VMEM((16, C), BF)
    s.n_up = pltpu.VMEM((TW, C), BF)
    s.n_upleft = pltpu.VMEM((TH, C), BF)
    s.p_down = pltpu.VMEM((TH, TW, C), BF)
    s.p_right = pltpu.VMEM((TH + 1, 16, C), BF)
    s.p_diag = pltpu.VMEM((TH, 16, C), BF)
    s.kcol = pltpu.VMEM((3, 32, C), BF)
    s.row0 = pltpu.VMEM((TW, C), BF)
    s.r_down = pltpu.VMEM((TH, TW, C), BF)
    s.r_right = pltpu.VMEM((TH + 1, 16, C), BF)
    s.r_diag = pltpu.VMEM((TH, 16, C), BF)
    s.r_k = pltpu.VMEM((8, 32, C), BF)
    s.r_row0 = pltpu.VMEM((TW, C), BF)
    s.r_s0 = pltpu.VMEM((16, C), BF)
    s.whole_t = pltpu.VMEM((C, 32 * PW), BF)
    s.fg_pad = pltpu.VMEM((FROWS, C), BF)
    s.x3f = pltpu.VMEM((FROWS, 3 * C), BF)
    s.wt = pltpu.VMEM((3, C, 3 * C), BF)
    s.parts = pltpu.VMEM((3, 4, 2, 4, 48, 128), BF)
    s.r0 = pltpu.VMEM((3, 4, 4, 48, 128), BF)
    s.a1 = pltpu.VMEM((3, 4, 4, 48, 128), BF)
    s.ra = pltpu.VMEM((3, 3, 4, 48, 128), BF)
    s.a2 = pltpu.VMEM((3, 4, 48, 128), BF)
    s.rb = pltpu.VMEM((3, 3, 48, 128), BF)
    s.a3 = pltpu.VMEM((3, 48, 128), BF)
    s.rz = pltpu.VMEM((3, 3, 48, 128), BF)
    s.canvas = pltpu.VMEM((2, 2 * TH, PW, 128), F32)
    s.wp = pltpu.VMEM((2, 46, 144, 128), F32)
    s.rl = pltpu.VMEM((32, 16, 256), F32)
    s.cl = pltpu.VMEM((32, 16, 256), F32)
    s.total = pltpu.VMEM((3, GR, 128), F32)
    s.by_z = pltpu.VMEM((4, 2, 48, 128), F32)
    s.metabuf = pltpu.VMEM((16, 8, 128), jnp.int32)
    s.meta_in = pltpu.VMEM((16, 8, 128), jnp.int32)
    s.smeta = pltpu.SMEM((16, 8, 128), jnp.int32)
    s.fetch = dma((5,))
    s.msend = dma((15,))
    s.mrecv = dma((15,))
    s.wsend = dma((15,))
    s.wrecv = dma((15,))
    s.asend = dma((15,))
    s.arecv = dma((15,))
    s.hsend = dma((8,))
    s.hrecv = dma((8,))
    s.keep = dma((4,))
    s.ssend = dma((4,))
    s.srecv = dma((4,))
    s.ysend = dma((6,))
    s.yrecv = dma((6,))
    s.tsend = dma((13,))
    s.trecv = dma((13,))
    s.csend = dma((3,))
    s.crecv = dma((3,))
    s.dsend = dma((9,))
    s.drecv = dma((9,))
    s.esend = dma((9,))
    s.erecv = dma((9,))
    s.zsend = dma((9,))
    s.zrecv = dma((9,))
    s.listed = dma(())
    s.vb = pltpu.VMEM((SPAN, C), BF)
    s.vx = pltpu.VMEM((SPAN, C), BF)
    s.vg = pltpu.VMEM((SPAN, C), BF)
    s.x3 = pltpu.VMEM((SPAN, 3 * C), BF)
    s.x3g = pltpu.VMEM((SPAN, 3 * C), BF)
    s.gt = pltpu.VMEM((C, 14 * LINE), BF)
    s.rgc_a = pltpu.VMEM((13, SA, C), BF)
    s.rgc_b = pltpu.VMEM((13, SB, C), BF)
    s.buf_a = pltpu.VMEM((16, 2, SA, C), BF)
    s.buf_b = pltpu.VMEM((16, 2, SB, C), BF)
    s.in_a = pltpu.VMEM((16, 2, SA, C), BF)
    s.in_b = pltpu.VMEM((16, 2, SB, C), BF)
    s.gbuf = pltpu.VMEM((256, C), BF)
    s.fetch0 = dma((9,))
    s.fetch1 = dma((9,))
    s.fetch2 = dma((9,))
    s.bsend = dma((15,))
    s.brecv = dma((15,))
    return pl.pallas_call(
        functools.partial(all_kernel, list(vars(s))),
        in_specs=[whole(None, pltpu.SMEM)] * 3 + [vm] * 2 + [hbm] * 8,
        out_specs=[vm] * 2,
        out_shape=[jax.ShapeDtypeStruct((TH, TW, C), BF), jax.ShapeDtypeStruct((3, 36, 128), F32)],
        scratch_shapes=list(vars(s).values()),
        compiler_params=pltpu.CompilerParams(vmem_limit_bytes=63 << 20, collective_id=1, has_side_effects=True),
        name="run_all",
    )(tgt, orow, ocol, rows, cols, pre, g2, feat, w2, w1, inp, grad, w)


def local(roi_feat, pre_one, grad_two, w_one, w_two, roi_rows, roi_cols, target_col, off_row, off_col, fpn_input, fpn_grad, w_fpn):
    grad_in, sums = run_all(
        target_col[:, 0], off_row, off_col, roi_rows, roi_cols, pre_one, grad_two, roi_feat, w_two, w_one, fpn_input, fpn_grad, w_fpn
    )
    return grad_in, sums[0].reshape(-1), sums[1].reshape(-1), sums[2].reshape(-1)


def solution(mesh):
    both = ("ty", "tx")
    placed = (
        P(both, None, None, None),
        P(both, None, None, None),
        P(both, None, None, None),
        P(),
        P(),
        P(both, None, None),
        P(both, None, None),
        P(both, None),
        P(both),
        P(both),
        P("ty", "tx", None),
        P("ty", "tx", None),
        P(),
    )
    return jax.shard_map(
        local,
        mesh=mesh,
        in_specs=placed,
        out_specs=(P("ty", "tx", None), P(both), P(both), P(both)),
        check_vma=False,
    )
```
